32 devices in a mesh: group: 4 (over y, x), bulk: 8 (over z, core).
Axes of the slice: x: 2, y: 2, z: 4, core: 2. Of those that a mesh axis runs over, the one named last changes fastest.
Arguments:
- right_sides: float32 [32, 65536], P(None, ('group', 'bulk')), may hold values from -6 to 6
- points: float32 [3, 65536], P(None, ('group', 'bulk')), may hold values from 0 to 4
- basis: float32 [256, 64, 256], P(('group', 'bulk')), may hold values from -0.375 to 0.375
- transfer: float32 [480, 64, 64], P(('group', 'bulk')), may hold values from -0.5 to 0.5
- skeleton: float32 [480, 3, 64], P(('group', 'bulk')), may hold values from 0 to 2
- near_list: int32 [256, 8], P(('group', 'bulk')), may hold values from 0 to 255, as said below
- near_count: int32 [256], P(('group', 'bulk')), may hold values from 0 to 8
- inter_list: int32 [480, 8], P(('group', 'bulk')), may hold values from 0 to 255, as said below
- inter_count: int32 [480], P(('group', 'bulk')), may hold values from 0 to 8
- upper_transfer: float32 [32, 64, 64], replicated, may hold values from -0.5 to 0.5
- upper_skeleton: float32 [32, 3, 64], replicated, may hold values from 0 to 2
- upper_list: int32 [32, 8], replicated, may hold values from 0 to 31, as said below
- upper_count: int32 [32], replicated, may hold values from 0 to 3, as said below
Outputs:
- product: float32 [32, 65536], P(None, ('group', 'bulk'))
The draws below stay inside these ranges and needn't reach their ends.
Inputs may be any that keep to these rules, and one draw needn't show every extreme that they name: `near_list`: row t holds distinct leaves other than t at most 4 leaves away; only the first near_count[t] entries count, the rest are in range and are ignored. `inter_list`: A node's row holds distinct other nodes of its level, each of the first inter_count entries at most max(m // 2, 1) places away where m is the level's nodes on one device; only the first inter_count entries count, the rest are in range and are ignored. `upper_list`: row h holds distinct other heap nodes of h's level; at levels with more nodes than there are indices of group, they lie below the same ancestor at the level that has one node per index of group. Only the first upper_count entries count, the rest are in range and are ignored. `upper_count`: entries 0 and 1 are 0.
All inputs are finite; a program needn't handle non-finite values.
Results may differ from the reference program's by a relative error of at most 0.0003.
Values sent between devices are 32-bit elements; how exact they have to be, the bound alone decides.
No kernel may reach another device: no remote copies, remote signals or barrier semaphores. Data moves between devices by JAX's collectives and lax.ppermute only.
A program may use at most 128 MiB of HBM per device.

```python
import jax
import jax.numpy as jnp
from jax import lax

LEAF = 256
RANK = 64
RHS = 32
NEAR = 8
NI = 8
LPD = 8
NL = 256
NPTS = 65536
LNODES = 480
HALF = 4
N_GROUP = 4
N_BULK = 8
DEVICES = 32


sheet_columns = 64


sheet_scale = 0.0625


sheet_depth = 0.5


def choose(base_key, sources, usable, limit, keep_count):
    row_count = sources.shape[0]
    candidate_count = sources.shape[1]
    score_key, count_key = jax.random.split(base_key)
    scores = jax.random.randint(score_key, (row_count, candidate_count), 0, 1 << 20) * candidate_count + jnp.arange(candidate_count)[None, :]
    scores = jnp.where(usable, scores, (1 << 20) * candidate_count + candidate_count)
    ordering = jnp.argsort(scores, axis=1, stable=True)[:, :keep_count]
    picked = jnp.take_along_axis(sources, ordering, axis=1)
    available = jnp.sum(usable.astype(jnp.int32), axis=1)
    wanted = jax.random.randint(count_key, (row_count,), 0, keep_count + 1)
    counts = jnp.minimum(jnp.minimum(wanted, limit), available)
    return (picked, counts)


def near_tables(key):
    base_key = jax.random.fold_in(key, 11)
    pick_key, dense_key = jax.random.split(base_key)
    offsets = jnp.concatenate([jnp.arange(-HALF, 0), jnp.arange(1, HALF + 1)])
    leaf_ids = jnp.arange(NL)
    sources = leaf_ids[:, None] + offsets[None, :]
    usable = (sources >= 0) & (sources < NL)
    density = jnp.repeat(jax.random.randint(dense_key, (DEVICES,), 1, NEAR + 1), LPD)
    picked, counts = choose(pick_key, sources, usable, density, NEAR)
    return (jnp.clip(picked, 0, NL - 1).astype(jnp.int32), counts.astype(jnp.int32))


def local_tables(key):
    base_key = jax.random.fold_in(key, 23)
    slot_count = 2 * LPD - 1
    node_rows = jnp.arange(DEVICES * slot_count)
    owner_device = node_rows // slot_count
    slot_index = node_rows % slot_count
    level_size = jnp.ones_like(node_rows)
    position = jnp.zeros_like(node_rows)
    for depth_level in range(LPD.bit_length()):
        node_count = LPD >> depth_level
        offset = 2 * LPD - 2 * node_count
        inside = (slot_index >= offset) & (slot_index < offset + node_count)
        level_size = jnp.where(inside, node_count, level_size)
        position = jnp.where(inside, slot_index - offset, position)
    reach_nodes = jnp.maximum(level_size // 2, 1)
    farthest = max(LPD // 2, 1)
    offsets = jnp.concatenate([jnp.arange(-farthest, 0), jnp.arange(1, farthest + 1)])
    global_index = owner_device * level_size + position
    sources = global_index[:, None] + offsets[None, :]
    level_end = DEVICES * level_size
    usable = (jnp.abs(offsets)[None, :] <= reach_nodes[:, None]) & (sources >= 0) & (sources < level_end[:, None])
    picked, counts = choose(base_key, sources, usable, NI, NI)
    picked = jnp.clip(picked, 0, (level_end - 1)[:, None])
    return (picked.astype(jnp.int32), counts.astype(jnp.int32))


def upper_tables(key):
    base_key = jax.random.fold_in(key, 37)
    heap_index = jnp.arange(DEVICES)
    top_levels = N_GROUP.bit_length() - 1
    depth_level = jnp.zeros_like(heap_index)
    for bit_power in range(1, DEVICES.bit_length() - 1):
        depth_level = depth_level + (heap_index >= 1 << bit_power).astype(depth_level.dtype)
    level_start = jnp.left_shift(1, depth_level)
    block_size = jnp.where(depth_level >= top_levels, jnp.left_shift(1, jnp.maximum(depth_level - top_levels, 0)), level_start)
    position = heap_index - level_start
    block_start = position // block_size * block_size
    widest = max(N_BULK // 2, NI)
    candidate = jnp.arange(widest)
    sources = level_start[:, None] + block_start[:, None] + candidate[None, :]
    usable = (candidate[None, :] < block_size[:, None]) & (sources != heap_index[:, None]) & (heap_index[:, None] >= 2)
    picked, counts = choose(base_key, sources, usable, NI, NI)
    last_available = jnp.sum(usable[DEVICES - 1].astype(jnp.int32))
    counts = counts.at[DEVICES - 1].set(jnp.minimum(last_available, NI))
    return (jnp.clip(picked, 0, DEVICES - 1).astype(jnp.int32), counts.astype(jnp.int32))


def draw_points(key, part):
    inside = jax.random.uniform(key, (3, NPTS), jnp.float32)
    upper_edge = float(max(4, NL // 1024))
    leaf_ids = jnp.arange(NPTS) // LEAF
    across = (leaf_ids % sheet_columns).astype(jnp.float32)
    along = (leaf_ids // sheet_columns).astype(jnp.float32)
    coord_x = sheet_scale * across + inside[0]
    coord_y = sheet_scale * along + inside[1]
    coord_z = sheet_depth * inside[2]
    return jnp.clip(jnp.stack([coord_x, coord_y, coord_z]), 0.0, upper_edge)


def draw_near_list(key, part):
    return near_tables(key)[0]


def draw_near_count(key, part):
    return near_tables(key)[1]


def draw_inter_list(key, part):
    return local_tables(key)[0]


def draw_inter_count(key, part):
    return local_tables(key)[1]


def draw_upper_list(key, part):
    return upper_tables(key)[0]


def draw_upper_count(key, part):
    return upper_tables(key)[1]


def block_scale(key, shape, pieces, smallest, largest):
    factor_of = 1.0
    for dim, blocks in pieces:
        draws = jax.random.uniform(jax.random.fold_in(jax.random.fold_in(key, 6), dim), (blocks,), jnp.float32, smallest / len(pieces), largest / len(pieces))
        factor_of = factor_of * jnp.repeat(jnp.exp(draws), shape[dim] // blocks).reshape((-1,) + (1,) * (len(shape) - 1 - dim))
    return factor_of


def gaussian(rng, dims, scale, reach, pieces=(), kind=jnp.bfloat16):
    factor_of = block_scale(rng, dims, pieces, -0.22, 0.18) if pieces else 1.0
    values = jax.random.normal(rng, dims, jnp.float32) * scale * factor_of
    return jnp.minimum(jnp.maximum(values, -reach), reach).astype(kind)


def setup_inputs(seed: int = 0) -> dict:
    streams_of = jax.random.split(jax.random.key(seed), 14)
    return {
        "right_sides": gaussian(streams_of[0], (RHS, NPTS), 1.0, 6.0, ((1, 32),), jnp.float32),
        "points": draw_points(jax.random.fold_in(streams_of[13], 71), 0),
        "basis": gaussian(streams_of[2], (NL, RANK, LEAF), LEAF ** -0.5, 0.375, ((0, 32),), jnp.float32),
        "transfer": gaussian(streams_of[3], (LNODES, RANK, RANK), (2 * RANK) ** -0.5, 0.5, ((0, 32),), jnp.float32),
        "skeleton": jnp.clip(2.0 * jax.random.uniform(streams_of[4], (LNODES, 3, RANK), jnp.float32) ** block_scale(streams_of[4], (LNODES, 3, RANK), ((0, 32),), -0.2, 0.2), 0.0, 2.0),
        "near_list": draw_near_list(jax.random.fold_in(streams_of[13], 71), 0),
        "near_count": draw_near_count(jax.random.fold_in(streams_of[13], 71), 0),
        "inter_list": draw_inter_list(jax.random.fold_in(streams_of[13], 71), 0),
        "inter_count": draw_inter_count(jax.random.fold_in(streams_of[13], 71), 0),
        "upper_transfer": gaussian(streams_of[9], (DEVICES, RANK, RANK), (2 * RANK) ** -0.5, 0.5, (), jnp.float32),
        "upper_skeleton": jnp.clip(jax.random.uniform(streams_of[10], (DEVICES, 3, RANK), jnp.float32, 0.0, 2.0), 0.0, 2.0),
        "upper_list": draw_upper_list(jax.random.fold_in(streams_of[13], 71), 0),
        "upper_count": draw_upper_count(jax.random.fold_in(streams_of[13], 71), 0),
    }


FULL_PRECISION = lax.Precision.HIGHEST
AMPLITUDE = 0.2
KERNEL_RATE = 2.0
SOFTENING = 0.01
NUGGET = 0.5

def matern(source_pts, target_pts):
    delta_x = source_pts[..., 0, :, None] - target_pts[..., 0, None, :]
    delta_y = source_pts[..., 1, :, None] - target_pts[..., 1, None, :]
    delta_z = source_pts[..., 2, :, None] - target_pts[..., 2, None, :]
    spread = jnp.sqrt(delta_x * delta_x + delta_y * delta_y + delta_z * delta_z + SOFTENING)
    scaled = KERNEL_RATE * spread
    return AMPLITUDE * (1.0 + scaled) * jnp.exp(-scaled)

def near_terms(own_points, own_rows, far_points, far_rows, weights):
    self_kernel = matern(own_points, own_points)
    result = jnp.einsum('brq,bqp->brp', own_rows, self_kernel, precision=FULL_PRECISION) + NUGGET * own_rows
    cross_kernel = matern(far_points, own_points[:, None])
    masked = far_rows * weights[:, :, None, None]
    return result + jnp.einsum('bnrq,bnqp->brp', masked, cross_kernel, precision=FULL_PRECISION)

def couple(skeleton_table, coef_table, positions, target_skeleton, counts):
    source_skeleton = jnp.take(skeleton_table, positions, axis=0)
    source_coefs = jnp.take(coef_table, positions, axis=0)
    kernel = matern(source_skeleton, target_skeleton[:, None])
    active = (jnp.arange(positions.shape[1])[None, :] < counts[:, None]).astype(jnp.float32)
    weighted = source_coefs * active[:, :, None, None]
    return jnp.einsum('nsri,nsij->nrj', weighted, kernel, precision=FULL_PRECISION)

def reference(right_sides, points, basis, transfer, skeleton, near_list, near_count, inter_list, inter_count, upper_transfer, upper_skeleton, upper_list, upper_count):
    points_leaf = points.reshape(3, NL, LEAF).transpose(1, 0, 2)
    rows_leaf = right_sides.reshape(RHS, NL, LEAF).transpose(1, 0, 2)
    weights = (jnp.arange(NEAR)[None, :] < near_count[:, None]).astype(jnp.float32)

    def near_block(first_leaf):
        own_points = lax.dynamic_slice_in_dim(points_leaf, first_leaf, LPD, 0)
        own_rows = lax.dynamic_slice_in_dim(rows_leaf, first_leaf, LPD, 0)
        source_ids = lax.dynamic_slice_in_dim(near_list, first_leaf, LPD, 0)
        block_weights = lax.dynamic_slice_in_dim(weights, first_leaf, LPD, 0)
        return near_terms(own_points, own_rows, jnp.take(points_leaf, source_ids, axis=0), jnp.take(rows_leaf, source_ids, axis=0), block_weights)
    near_part = lax.map(near_block, jnp.arange(0, NL, LPD, dtype=jnp.int32)).reshape(NL, RHS, LEAF)
    slot_count = 2 * LPD - 1
    transfer_dev = transfer.reshape(DEVICES, slot_count, RANK, RANK)
    skeleton_dev = skeleton.reshape(DEVICES, slot_count, 3, RANK)
    list_dev = inter_list.reshape(DEVICES, slot_count, NI)
    count_dev = inter_count.reshape(DEVICES, slot_count)
    level_total = LPD.bit_length()

    def level_portion(values, level_index):
        node_count = LPD >> level_index
        offset = 2 * LPD - 2 * node_count
        portion = values[:, offset:offset + node_count]
        return portion.reshape((DEVICES * node_count,) + portion.shape[2:])
    coefficients = [jnp.einsum('lrp,lkp->lrk', rows_leaf, basis, precision=FULL_PRECISION)]
    for level_index in range(level_total - 1):
        lifted = jnp.einsum('nrk,nkq->nrq', coefficients[-1], level_portion(transfer_dev, level_index), precision=FULL_PRECISION)
        coefficients.append(lifted.reshape(-1, 2, RHS, RANK).sum(axis=1))
    root_transfer = transfer_dev[:, slot_count - 1]
    root_terms = jnp.einsum('nrk,nkq->nrq', coefficients[-1], root_transfer, precision=FULL_PRECISION)
    local_fields = []
    for level_index in range(level_total):
        skeleton_here = level_portion(skeleton_dev, level_index)
        local_fields.append(couple(skeleton_here, coefficients[level_index], level_portion(list_dev, level_index), skeleton_here, level_portion(count_dev, level_index)))
    tree_depth = DEVICES.bit_length() - 1
    level_coef = root_terms.reshape(-1, 2, RHS, RANK).sum(axis=1)
    heap_parts = []
    for level_index in range(tree_depth - 1, 0, -1):
        heap_parts.insert(0, level_coef)
        if level_index > 1:
            lifted = jnp.einsum('nrk,nkq->nrq', level_coef, upper_transfer[1 << level_index:2 << level_index], precision=FULL_PRECISION)
            level_coef = lifted.reshape(-1, 2, RHS, RANK).sum(axis=1)
    heap_coefs = jnp.concatenate([jnp.zeros((2, RHS, RANK), jnp.float32)] + heap_parts, axis=0)
    upper_fields = couple(upper_skeleton, heap_coefs, upper_list, upper_skeleton, upper_count)
    downward = upper_fields[2:4]
    for level_index in range(2, tree_depth):
        parent = jnp.repeat(downward, 2, axis=0)
        downward = upper_fields[1 << level_index:2 << level_index] + jnp.einsum('nrq,nkq->nrk', parent, upper_transfer[1 << level_index:2 << level_index], precision=FULL_PRECISION)
    incoming = jnp.einsum('nrq,nkq->nrk', jnp.repeat(downward, 2, axis=0), root_transfer, precision=FULL_PRECISION)
    local_fields[-1] = local_fields[-1] + incoming
    for level_index in range(level_total - 2, -1, -1):
        parent = jnp.repeat(local_fields[level_index + 1], 2, axis=0)
        local_fields[level_index] = local_fields[level_index] + jnp.einsum('nrq,nkq->nrk', parent, level_portion(transfer_dev, level_index), precision=FULL_PRECISION)
    far_part = jnp.einsum('lrk,lkp->rlp', local_fields[0], basis, precision=FULL_PRECISION)
    combined = far_part + near_part.transpose(1, 0, 2)
    return combined.reshape(RHS, NPTS)
```

```python
import functools
import math

import jax
import jax.numpy as jnp
from jax import lax
from jax.experimental import pallas as pl
from jax.experimental.pallas import tpu as pltpu
from jax.sharding import PartitionSpec as P

AMPLITUDE = 0.2
KERNEL_RATE = 2.0
SOFTENING = 0.01
NUGGET = 0.5
SCALE = KERNEL_RATE * math.log2(math.e)
FLOOR = SOFTENING * SCALE * SCALE
SHIFT = 1.0 / math.log(2.0)
GAIN = AMPLITUDE * math.log(2.0)
FEATURES = 48
STEP = 4
AXES = ("group", "bulk")

f32 = jnp.float32
bf16 = jnp.bfloat16


def dot(a, b, ca, cb):
    return lax.dot_general(a, b, (((ca,), (cb,)), ((), ())), preferred_element_type=f32)


def split2(x):
    high = x.astype(bf16)
    return high, (x - high.astype(f32)).astype(bf16)


def split3(x):
    a = x.astype(bf16).astype(f32)
    b = (x - a).astype(bf16).astype(f32)
    return a, b, x - a - b


def matmul(a, b, ca=1, cb=0):
    ah, al = split2(a)
    bh, bl = split2(b)
    rows = a.shape[1 - ca]
    if ca == 1:
        both = dot(jnp.concatenate([ah, al], axis=0), bh, ca, cb)
        return both[:rows] + both[rows:] + dot(ah, bl, ca, cb)
    return dot(ah, bh, ca, cb) + dot(al, bh, ca, cb) + dot(ah, bl, ca, cb)


def scaled_points(coords):
    u = coords * SCALE
    return u, jnp.broadcast_to(jnp.sum(u * u, axis=0, keepdims=True), u.shape)


def place(row, vector, first, second, third):
    rest = jnp.where(row == 5, third, 0.0)
    rest = jnp.where(row == 4, second, rest)
    rest = jnp.where(row == 3, first, rest)
    return jnp.where(row < 3, vector, rest)


def source_features(coords):
    u, length = scaled_points(coords)
    row = lax.broadcasted_iota(jnp.int32, u.shape, 0)
    a, b, c = split3(u)
    return jnp.concatenate(
        [place(row, a, *split3(length)), place(row, a, 1.0, 1.0, 1.0), b, b, a, c], axis=0
    )


def target_features(coords):
    u, length = scaled_points(coords)
    row = lax.broadcasted_iota(jnp.int32, u.shape, 0)
    a, b, c = split3(-2.0 * u)
    return jnp.concatenate(
        [place(row, a, 1.0, 1.0, 1.0), place(row, b, *split3(length + FLOOR)), a, b, c, a], axis=0
    )


def kernel_of(square):
    t = square * lax.rsqrt(square)
    return (SHIFT + t) * jnp.exp2(-t)


def halves(nodes):
    return max(nodes // 2, 1)


class Sizes:
    def __init__(self, mesh_group, mesh_bulk, leaves, rank, leaf, rhs, near, slots):
        self.group, self.bulk = mesh_group, mesh_bulk
        self.devices = mesh_group * mesh_bulk
        self.leaves, self.rank, self.leaf, self.rhs = leaves, rank, leaf, rhs
        self.near, self.slots = near, slots
        self.levels = leaves.bit_length()
        self.counts = [leaves >> level for level in range(self.levels)]
        self.offsets = [2 * leaves - 2 * count for count in self.counts]
        self.nodes = 2 * leaves - 1
        self.depth = self.devices.bit_length() - 1
        self.top = mesh_group.bit_length() - 1
        self.half = halves(leaves)
        self.message_c = []
        at = self.half * leaf
        for count in self.counts:
            self.message_c.append(at)
            at += halves(count) * rank
        at = -(-at // 128) * 128
        self.message_terms = at
        self.terms = self.depth - self.top
        at += self.terms * rank
        self.message = -(-at // 128) * 128
        self.ext_counts = [count + 2 * halves(count) for count in self.counts]
        self.ext_offsets = [sum(self.ext_counts[:i]) for i in range(self.levels)]
        self.ext_nodes = sum(self.ext_counts)


def put(ref, rows, at, value):
    ref[rows, at : at + value.shape[1]] = value


def up_kernel(z, info, rhs_ref, pts_ref, basis_ref, transfer_ref, skel_ref, *rest):
    upper = rest[: z.terms - 1]
    near_ref, far_ref, coef_ref, terms_ref = rest[z.terms - 1 :]
    parity = info[0] % 2
    rows = slice(0, z.rhs)
    spare = slice(z.rhs, z.rhs + 8)
    pair = 2 * z.rank
    tables = []
    pieces = []
    for leaf in range(z.leaves):
        at = leaf * z.leaf
        pieces.append(matmul(rhs_ref[:, at : at + z.leaf], basis_ref[leaf], 1, 1))
    for level in range(z.levels):
        tables.append(pieces)
        for i, piece in enumerate(pieces):
            coef_ref[z.offsets[level] + i] = piece
        if level + 1 < z.levels:
            raised = []
            for i in range(z.counts[level + 1]):
                both = jnp.concatenate([pieces[2 * i], pieces[2 * i + 1]], axis=1)
                first = z.offsets[level] + 2 * i
                matrix = transfer_ref[first : first + 2].reshape(pair, z.rank)
                raised.append(matmul(both, matrix))
            pieces = raised
    term = matmul(tables[-1][0], transfer_ref[z.nodes - 1])
    lifted = [term]
    for matrix in upper:
        term = matmul(term, matrix[0])
        lifted.append(term)
    terms_ref[...] = jnp.concatenate(lifted, axis=1)
    width = z.half * z.leaf
    for ref, flip in ((near_ref, 0), (far_ref, 1)):
        last = (parity + 1 + flip) % 2
        at = pl.multiple_of(last * ((z.leaves - z.half) * z.leaf), 128)
        ref[rows, 0:width] = rhs_ref[:, pl.ds(at, width)]
        ref[spare, :] = jnp.zeros((8, z.message), f32)
        ref[z.rhs : z.rhs + 3, 0:width] = pts_ref[:, pl.ds(at, width)]
        for level in range(z.levels):
            count, start = z.counts[level], z.message_c[level]
            shift = count - halves(count)
            for i in range(halves(count)):
                node = z.offsets[level] + i + last * shift
                here = slice(start + i * z.rank, start + (i + 1) * z.rank)
                ref[rows, here] = coef_ref[node]
                ref[z.rhs : z.rhs + 3, here] = skel_ref[node]
        ref[rows, z.message_terms : z.message_terms + z.terms * z.rank] = terms_ref[...]


def near_kernel(z, info, list_ref, count_ref, rhs_ref, pts_ref, a_ref, b_ref, out_ref, src, tgt, val, halo):
    device = info[0]
    parity = device % 2
    width = z.half * z.leaf

    @pl.when(parity == 0)
    def _():
        halo[0] = b_ref[:, 0:width]
        halo[1] = a_ref[:, 0:width]

    @pl.when(parity == 1)
    def _():
        halo[0] = a_ref[:, 0:width]
        halo[1] = b_ref[:, 0:width]

    def fill(first, values, coords):
        high, low = split2(values * GAIN)
        features = source_features(coords)
        for i in range(values.shape[1] // z.leaf):
            here = slice(i * z.leaf, (i + 1) * z.leaf)
            val[first + i, 0 : z.rhs] = high[:, here]
            val[first + i, z.rhs : 2 * z.rhs] = low[:, here]
            src[first + i] = features[:, here].T.astype(bf16)

    coords = jnp.concatenate([pts_ref[...], jnp.zeros((5, pts_ref.shape[1]), f32)], axis=0)
    fill(0, halo[0, 0 : z.rhs], halo[0, z.rhs : z.rhs + 8])
    fill(z.half, rhs_ref[...], coords)
    fill(z.half + z.leaves, halo[1, 0 : z.rhs], halo[1, z.rhs : z.rhs + 8])
    features = target_features(coords).astype(bf16)
    for i in range(z.leaves):
        tgt[i] = features[:, i * z.leaf : (i + 1) * z.leaf]
    last = 2 * z.half + z.leaves - 1

    def term(target, source, weight):
        kernel_high, kernel_low = split2(kernel_of(dot(src[source], tgt[target], 1, 0)))
        values = val[source]
        both = dot(values, kernel_high, 1, 0)
        total = both[: z.rhs] + both[z.rhs :] + dot(values[: z.rhs], kernel_low, 1, 0)
        return total if weight is None else total * weight

    def one(target, carry):
        count = count_ref[target]

        def body(i, total):
            for k in range(STEP):
                slot = i * STEP + k
                source = list_ref[target, jnp.minimum(slot, z.near - 1)] - device * z.leaves + z.half
                source = jnp.clip(source, 0, last)
                total += term(target, source, jnp.where(slot < count, 1.0, 0.0))
            return total

        total = term(target, target + z.half, None)
        halo[0, 0 : z.rhs, 0 : z.leaf] = lax.fori_loop(0, (count + STEP - 1) // STEP, body, total)
        at = pl.multiple_of(target * z.leaf, 128)
        out_ref[:, pl.ds(at, z.leaf)] = halo[0, 0 : z.rhs, 0 : z.leaf] + NUGGET * rhs_ref[:, pl.ds(at, z.leaf)]
        return carry

    lax.fori_loop(0, z.leaves, one, 0)


def pad8(block):
    return jnp.concatenate([block, jnp.zeros((8 - block.shape[0], block.shape[1]), f32)], axis=0)


def gathered_kernel(z, sources, target_rows):
    return split2(kernel_of(dot(target_rows, sources, 1, 0)))


def packed(blocks):
    return blocks[0] if len(blocks) == 1 else jnp.concatenate(blocks, axis=1)


def couple(kernel_high, kernel_low, coefs):
    high, low = split2(coefs)
    rows = coefs.shape[0]
    both = dot(jnp.concatenate([high, low], axis=0), kernel_high, 1, 1)
    return both[:rows] + both[rows:] + dot(high, kernel_low, 1, 1)


def local_kernel(z, info, list_ref, count_ref, coef_ref, skel_ref, a_ref, b_ref, out_ref, table, feats, halo):
    device = info[0]
    parity = device % 2
    start = z.message_c[0]

    @pl.when(parity == 0)
    def _():
        halo[0] = b_ref[...]
        halo[1] = a_ref[...]

    @pl.when(parity == 1)
    def _():
        halo[0] = a_ref[...]
        halo[1] = b_ref[...]

    row_features = []
    for level in range(z.levels):
        count, half, base = z.counts[level], halves(z.counts[level]), z.ext_offsets[level]
        for i in range(half):
            here = slice(z.message_c[level] + i * z.rank, z.message_c[level] + (i + 1) * z.rank)
            for side, first in ((0, base), (1, base + half + count)):
                table[first + i] = halo[side, 0 : z.rhs, here] * GAIN
                feats[first + i] = source_features(halo[side, z.rhs : z.rhs + 8, here])
        for i in range(count):
            node = z.offsets[level] + i
            table[base + half + i] = coef_ref[node] * GAIN
            coords = pad8(skel_ref[node])
            feats[base + half + i] = source_features(coords)
            row_features.append(target_features(coords).T.astype(bf16))
    for level in range(z.levels):
        count, half, base = z.counts[level], halves(z.counts[level]), z.ext_offsets[level]
        for i in range(count):
            node = z.offsets[level] + i
            used = count_ref[node]
            values, points = [], []
            for slot in range(z.slots):
                at = jnp.clip(list_ref[node, slot] - device * count + half, 0, z.ext_counts[level] - 1)
                values.append(table[base + at] * jnp.where(slot < used, 1.0, 0.0))
                points.append(feats[base + at])
            high, low = gathered_kernel(z, packed(points).astype(bf16), row_features[node])
            out_ref[node] = couple(high, low, packed(values))


def final_kernel(z, info, list_ref, count_ref, near_ref, field_ref, basis_ref, transfer_ref, skel_ref, matrix_ref, *rest):
    tables, out_ref = rest[: z.terms], rest[-1]
    device = info[0]
    values = {}
    for i in range(z.terms):
        table = tables[i]
        values[z.depth - 1 - i] = table
    top = values[z.top]
    size = z.group
    own = (z.devices + device) >> (z.depth - z.top)
    level_values = {}
    current = [top[j] for j in range(size)]
    level_values[z.top] = current
    for level in range(z.top, 1, -1):
        anchor = (z.devices + device) >> (z.depth - level)
        moved = [matmul(current[j], matrix_ref[anchor ^ j]) for j in range(len(current))]
        current = [moved[2 * j] + moved[2 * j + 1] for j in range(len(current) // 2)]
        level_values[level - 1] = current
    downward = None
    for level in range(1, z.depth):
        anchor = (z.devices + device) >> (z.depth - level)
        if level <= z.top:
            size = len(level_values[level])
        else:
            size = z.bulk >> (z.depth - level)
        used = count_ref[anchor]
        slots = min(z.slots, size - 1)
        if slots:
            target = target_features(pad8(skel_ref[anchor])).T.astype(bf16)
            coefs, points = [], []
            for slot in range(slots):
                source = list_ref[anchor, slot]
                at = jnp.where(slot < used, source ^ anchor, 0)
                source = jnp.where(slot < used, source, anchor)
                weight = jnp.where(slot < used, GAIN, 0.0)
                if level < z.top:
                    chosen = level_values[level][0] * 0.0
                    for j in range(1, size):
                        chosen += level_values[level][j] * jnp.where(at == j, weight, 0.0)
                else:
                    chosen = values[level][at] * weight
                coefs.append(chosen)
                points.append(source_features(pad8(skel_ref[source])))
            high, low = gathered_kernel(z, packed(points).astype(bf16), target)
            field = couple(high, low, packed(coefs))
        else:
            field = jnp.zeros((z.rhs, z.rank), f32)
        if downward is None:
            downward = field
        else:
            downward = field + matmul(downward, matrix_ref[anchor], 1, 1)
    incoming = matmul(downward, transfer_ref[z.nodes - 1], 1, 1)
    fields = [field_ref[z.nodes - 1] + incoming]
    for level in range(z.levels - 2, -1, -1):
        below = []
        for i in range(z.counts[level]):
            node = z.offsets[level] + i
            below.append(field_ref[node] + matmul(fields[i // 2], transfer_ref[node], 1, 1))
        fields = below
    for leaf in range(z.leaves):
        here = slice(leaf * z.leaf, (leaf + 1) * z.leaf)
        out_ref[:, here] = near_ref[:, here] + matmul(fields[leaf], basis_ref[leaf])


SMEM = pl.BlockSpec(memory_space=pltpu.SMEM)
VMEM = pl.BlockSpec(memory_space=pltpu.VMEM)


def flip(x, axis, bit):
    return lax.ppermute(x, axis, [(i, i ^ bit) for i in range(lax.axis_size(axis))])


def on_device(
    right_sides,
    points,
    basis,
    transfer,
    skeleton,
    near_list,
    near_count,
    inter_list,
    inter_count,
    upper_transfer,
    upper_skeleton,
    upper_list,
    upper_count,
):
    z = Sizes(
        lax.axis_size("group"),
        lax.axis_size("bulk"),
        basis.shape[0],
        basis.shape[1],
        basis.shape[2],
        right_sides.shape[0],
        near_list.shape[1],
        inter_list.shape[1],
    )
    device = lax.axis_index(AXES).astype(jnp.int32)
    info = device.reshape(1)
    message = jax.ShapeDtypeStruct((z.rhs + 8, z.message), f32)

    def ancestor(level):
        return lambda i, info: ((z.devices + info[0]) // (1 << (z.depth - level)), 0, 0)

    def whole(array):
        return pl.BlockSpec(array.shape, lambda i, info, n=array.ndim: (0,) * n)

    raised = [upper_transfer] * (z.terms - 1)
    outs = (
        message,
        message,
        jax.ShapeDtypeStruct((z.nodes, z.rhs, z.rank), f32),
        jax.ShapeDtypeStruct((z.rhs, z.terms * z.rank), f32),
    )
    to_partner, to_other, coefs, terms = pl.pallas_call(
        functools.partial(up_kernel, z),
        name="up",
        out_shape=outs,
        grid_spec=pltpu.PrefetchScalarGridSpec(
            num_scalar_prefetch=1,
            grid=(1,),
            in_specs=[whole(a) for a in (right_sides, points, basis, transfer, skeleton)]
            + [
                pl.BlockSpec((1, z.rank, z.rank), ancestor(level))
                for level in range(z.depth - 1, z.top, -1)
            ],
            out_specs=[whole(a) for a in outs],
        ),
    )(info, right_sides, points, basis, transfer, skeleton, *raised)
    from_partner = flip(to_partner, "bulk", 1)
    pairs = [(i, i + 1) for i in range(1, z.devices - 1, 2)]
    from_other = lax.ppermute(to_other, AXES, pairs + [(b, a) for a, b in pairs])

    near_part = pl.pallas_call(
        functools.partial(near_kernel, z),
        name="near",
        out_shape=jax.ShapeDtypeStruct(right_sides.shape, f32),
        in_specs=[SMEM, SMEM, SMEM, VMEM, VMEM, VMEM, VMEM],
        out_specs=VMEM,
        scratch_shapes=[
            pltpu.VMEM((2 * z.half + z.leaves, z.leaf, FEATURES), bf16),
            pltpu.VMEM((z.leaves, FEATURES, z.leaf), bf16),
            pltpu.VMEM((2 * z.half + z.leaves, 2 * z.rhs, z.leaf), bf16),
            pltpu.VMEM((2, z.rhs + 8, z.half * z.leaf), f32),
        ],
    )(info, near_list, near_count, right_sides, points, from_partner, from_other)

    fields = pl.pallas_call(
        functools.partial(local_kernel, z),
        name="local",
        out_shape=jax.ShapeDtypeStruct((z.nodes, z.rhs, z.rank), f32),
        in_specs=[SMEM, SMEM, SMEM, VMEM, VMEM, VMEM, VMEM],
        out_specs=VMEM,
        scratch_shapes=[
            pltpu.VMEM((z.ext_nodes, z.rhs, z.rank), f32),
            pltpu.VMEM((z.ext_nodes, FEATURES, z.rank), f32),
            pltpu.VMEM((2, z.rhs + 8, z.message), f32),
        ],
    )(info, inter_list, inter_count, coefs, skeleton, from_partner, from_other)

    first = z.message_terms
    terms = terms.reshape(z.rhs, z.terms, z.rank).transpose(1, 0, 2)
    theirs = from_partner[: z.rhs, first : first + z.terms * z.rank]
    theirs = theirs.reshape(z.rhs, z.terms, z.rank).transpose(1, 0, 2)
    whole_levels, partial = [], terms + theirs
    for bit in range(1, z.bulk.bit_length()):
        whole_levels.append(partial[:1])
        partial = partial[1:]
        if bit == z.bulk.bit_length() - 1:
            break
        sizes = [level.shape[0] for level in whole_levels]
        sent = jnp.concatenate(whole_levels + [partial], axis=0)
        received = flip(sent, "bulk", 1 << bit)
        at = 0
        for i, size in enumerate(sizes):
            whole_levels[i] = jnp.concatenate([whole_levels[i], received[at : at + size]], axis=0)
            at += size
        partial = partial + received[at:]
    top = whole_levels[-1]
    for bit in range(z.top):
        top = jnp.concatenate([top, flip(top, "group", 1 << bit)], axis=0)
    whole_levels[-1] = top

    return pl.pallas_call(
        functools.partial(final_kernel, z),
        name="final",
        out_shape=jax.ShapeDtypeStruct(right_sides.shape, f32),
        in_specs=[SMEM, SMEM, SMEM] + [VMEM] * (6 + z.terms),
        out_specs=VMEM,
    )(
        info,
        upper_list,
        upper_count,
        near_part,
        fields,
        basis,
        transfer,
        upper_skeleton,
        upper_transfer,
        *whole_levels,
    )


def solution(mesh):
    in_specs = (
        P(None, AXES),
        P(None, AXES),
        P(AXES, None, None),
        P(AXES, None, None),
        P(AXES, None, None),
        P(AXES, None),
        P(AXES),
        P(AXES, None),
        P(AXES),
        P(),
        P(),
        P(),
        P(),
    )
    return jax.shard_map(
        on_device, mesh=mesh, in_specs=in_specs, out_specs=P(None, AXES), check_vma=False
    )
```

```python
import functools
import math

import jax
import jax.numpy as jnp
from jax import lax
from jax.experimental import pallas as pl
from jax.experimental.pallas import tpu as pltpu
from jax.sharding import PartitionSpec as P

AMPLITUDE = 0.2
KERNEL_RATE = 2.0
SOFTENING = 0.01
NUGGET = 0.5
SCALE = KERNEL_RATE * math.log2(math.e)
FLOOR = SOFTENING * SCALE * SCALE
SHIFT = 1.0 / math.log(2.0)
GAIN = AMPLITUDE * math.log(2.0)
FEATURES = 48
STEP = 4
NEAR_SHARES = (5, 10, 13)
AXES = ("group", "bulk")

f32 = jnp.float32
bf16 = jnp.bfloat16


def dot(a, b, ca, cb):
    return lax.dot_general(a, b, (((ca,), (cb,)), ((), ())), preferred_element_type=f32)


def split2(x):
    high = x.astype(bf16)
    return high, (x - high.astype(f32)).astype(bf16)


def split3(x):
    a = x.astype(bf16).astype(f32)
    b = (x - a).astype(bf16).astype(f32)
    return a, b, x - a - b


def matmul(a, b, ca=1, cb=0):
    ah, al = split2(a)
    bh, bl = split2(b)
    rows = a.shape[1 - ca]
    if ca == 1:
        both = dot(jnp.concatenate([ah, al], axis=0), bh, ca, cb)
        return both[:rows] + both[rows:] + dot(ah, bl, ca, cb)
    return dot(ah, bh, ca, cb) + dot(al, bh, ca, cb) + dot(ah, bl, ca, cb)


def scaled_points(coords):
    u = coords * SCALE
    return u, jnp.broadcast_to(jnp.sum(u * u, axis=0, keepdims=True), u.shape)


def place(row, vector, first, second, third):
    rest = jnp.where(row == 5, third, 0.0)
    rest = jnp.where(row == 4, second, rest)
    rest = jnp.where(row == 3, first, rest)
    return jnp.where(row < 3, vector, rest)


def source_features(coords):
    u, length = scaled_points(coords)
    row = lax.broadcasted_iota(jnp.int32, u.shape, 0)
    a, b, c = split3(u)
    return jnp.concatenate(
        [place(row, a, *split3(length)), place(row, a, 1.0, 1.0, 1.0), b, b, a, c], axis=0
    )


def target_features(coords):
    u, length = scaled_points(coords)
    row = lax.broadcasted_iota(jnp.int32, u.shape, 0)
    a, b, c = split3(-2.0 * u)
    return jnp.concatenate(
        [place(row, a, 1.0, 1.0, 1.0), place(row, b, *split3(length + FLOOR)), a, b, c, a], axis=0
    )


def kernel_of(square):
    t = square * lax.rsqrt(square)
    return (SHIFT + t) * jnp.exp2(-t)


def halves(nodes):
    return max(nodes // 2, 1)


class Sizes:
    def __init__(self, mesh_group, mesh_bulk, leaves, rank, leaf, rhs, near, slots):
        self.group, self.bulk = mesh_group, mesh_bulk
        self.devices = mesh_group * mesh_bulk
        self.leaves, self.rank, self.leaf, self.rhs = leaves, rank, leaf, rhs
        self.near, self.slots = near, slots
        self.levels = leaves.bit_length()
        self.counts = [leaves >> level for level in range(self.levels)]
        self.offsets = [2 * leaves - 2 * count for count in self.counts]
        self.nodes = 2 * leaves - 1
        self.depth = self.devices.bit_length() - 1
        self.top = mesh_group.bit_length() - 1
        self.half = halves(leaves)
        self.message_c = []
        at = self.half * leaf
        for count in self.counts:
            self.message_c.append(at)
            at += halves(count) * rank
        self.message_term = -(-at // 128) * 128
        self.message = self.message_term + -(-rank // 128) * 128
        self.packed = -(-self.nodes * rank // 128) * 128
        self.ext_counts = [count + 2 * halves(count) for count in self.counts]
        self.ext_offsets = [sum(self.ext_counts[:i]) for i in range(self.levels)]
        self.ext_nodes = sum(self.ext_counts)
        self.upper_levels = list(range(1, self.depth))

    def level_size(self, level):
        return self.bulk >> (self.depth - level) if level > self.top else 1 << level

    def level_slots(self, level):
        return min(self.slots, self.level_size(level) - 1)

    def anchor(self, device, level):
        return (self.devices + device) >> (self.depth - level)


def up_kernel(
    z, info_ref, near_list, near_count, inter_list, inter_count, upper_list, upper_count,
    rhs_ref, pts_ref, basis_ref, transfer_ref, skel_ref,
    near_msg, far_msg, own_ref, term_ref, items_ref, halo_ref, bounds_ref, slots_ref, upper_ref,
):
    device = info_ref[0]
    parity = device % 2
    pair = 2 * z.rank
    rows, spare = slice(0, z.rhs), slice(z.rhs, z.rhs + 8)
    coords = slice(z.rhs, z.rhs + 3)
    own_ref[spare, :] = jnp.zeros((8, z.packed), f32)
    for node in range(z.nodes):
        own_ref[coords, node * z.rank : (node + 1) * z.rank] = skel_ref[:, node, :]
    pieces = []
    for leaf in range(z.leaves):
        at = leaf * z.leaf
        pieces.append(matmul(rhs_ref[:, at : at + z.leaf], basis_ref[leaf], 1, 1))
    for level in range(z.levels):
        first = z.offsets[level]
        if len(pieces) == 1:
            own_ref[rows, first * z.rank : (first + 1) * z.rank] = pieces[0]
            break
        raised = []
        for i in range(len(pieces) // 2):
            both = jnp.concatenate([pieces[2 * i], pieces[2 * i + 1]], axis=1)
            node = first + 2 * i
            own_ref[rows, node * z.rank : node * z.rank + pair] = both
            raised.append(matmul(both, transfer_ref[node : node + 2].reshape(pair, z.rank)))
        pieces = raised
    term = matmul(pieces[0], transfer_ref[z.nodes - 1])
    term_ref[...] = term
    width = z.half * z.leaf
    for ref, other in ((near_msg, 0), (far_msg, 1)):
        last = (parity + 1 + other) % 2
        at = pl.multiple_of(last * ((z.leaves - z.half) * z.leaf), 128)
        ref[spare, :] = jnp.zeros((8, z.message), f32)
        ref[rows, 0:width] = rhs_ref[:, pl.ds(at, width)]
        ref[coords, 0:width] = pts_ref[:, pl.ds(at, width)]
        for level in range(z.levels):
            size = halves(z.counts[level]) * z.rank
            first = z.offsets[level] * z.rank
            shift = (z.counts[level] - halves(z.counts[level])) * z.rank
            here = slice(z.message_c[level], z.message_c[level] + size)
            low = own_ref[:, first : first + size]
            if shift:
                low = jnp.where(last == 1, own_ref[:, first + shift : first + shift + size], low)
            ref[:, here] = low
        ref[rows, z.message_term : z.message_term + z.rank] = term

    here = z.leaves
    for leaf in range(z.leaves):
        items_ref[leaf] = leaf * (z.leaves + 1)
    away = 0
    for leaf in range(z.leaves):
        count = near_count[leaf]
        for slot in range(z.near):
            source = near_list[leaf, slot] - device * z.leaves
            used = jnp.where(slot < count, 1, 0)
            inside = jnp.where((source >= 0) & (source < z.leaves), used, 0)
            items_ref[here] = leaf * z.leaves + jnp.clip(source, 0, z.leaves - 1)
            place_in_halo = jnp.where(source < 0, source + z.half, source - z.leaves + z.half)
            halo_ref[away] = leaf * 2 * z.half + jnp.clip(place_in_halo, 0, 2 * z.half - 1)
            here = here + inside
            away = away + used - inside
    bounds_ref[0] = here
    bounds_ref[1] = away
    bounds_ref[2] = device
    for level in range(z.levels):
        count, half, base = z.counts[level], halves(z.counts[level]), z.ext_offsets[level]
        for i in range(count):
            node = z.offsets[level] + i
            for slot in range(z.slots):
                at = inter_list[slot, node] - device * count + half
                slots_ref[node * z.slots + slot] = base + jnp.clip(at, 0, z.ext_counts[level] - 1)
            bounds_ref[3 + node] = inter_count[node]
    for k, level in enumerate(z.upper_levels):
        anchor = z.anchor(device, level)
        used = upper_count[anchor]
        for slot in range(z.level_slots(level)):
            upper_ref[k * z.slots + slot] = jnp.where(slot < used, upper_list[slot, anchor], -1)


def pair_kernel(z, bounds_ref, term_ref, a_ref, matrix_ref, out_ref):
    device = bounds_ref[2]
    term = term_ref[...] + a_ref[0 : z.rhs, z.message_term : z.message_term + z.rank]
    out_ref[0] = term
    for i, level in enumerate(range(z.depth - 1, z.top, -1)):
        term = matmul(term, matrix_ref[z.anchor(device, level)])
        out_ref[i + 1] = term


def pad8(block):
    return jnp.concatenate([block, jnp.zeros((8 - block.shape[0], block.shape[1]), f32)], axis=0)


def fill_sources(z, src, val, first, values, coords):
    high, low = split2(values * GAIN)
    features = source_features(coords)
    for i in range(values.shape[1] // z.leaf):
        here = slice(i * z.leaf, (i + 1) * z.leaf)
        val[first + i, 0 : z.rhs] = high[:, here]
        val[first + i, z.rhs : 2 * z.rhs] = low[:, here]
        src[first + i] = features[:, here].T.astype(bf16)


def own_kernel(z, rhs_ref, pts_ref, src, tgt, val, acc):
    coords = pad8(pts_ref[...])
    fill_sources(z, src, val, 0, rhs_ref[...], coords)
    features = target_features(coords).astype(bf16)
    for i in range(z.leaves):
        here = slice(i * z.leaf, (i + 1) * z.leaf)
        tgt[i] = features[:, here]
        acc[i] = NUGGET * rhs_ref[:, here]


def halo_kernel(z, bounds_ref, a_ref, b_ref, src, val):
    width = z.half * z.leaf
    parity = bounds_ref[2] % 2
    left = jnp.where(parity == 0, b_ref[:, 0:width], a_ref[:, 0:width])
    right = jnp.where(parity == 0, a_ref[:, 0:width], b_ref[:, 0:width])
    fill_sources(z, src, val, 0, left[0 : z.rhs], left[z.rhs : z.rhs + 8])
    fill_sources(z, src, val, z.half, right[0 : z.rhs], right[z.rhs : z.rhs + 8])


def run_items(z, list_ref, per_target, first, end, src, tgt, val, acc):
    def group(at, size):
        for k in range(size):
            item = list_ref[at + k]
            target, source = item // per_target, item % per_target
            kernel_high, kernel_low = split2(kernel_of(dot(src[source], tgt[target], 1, 0)))
            values = val[source]
            both = dot(values, kernel_high, 1, 0)
            low = dot(values[: z.rhs], kernel_low, 1, 0)
            acc[target] += both[: z.rhs] + both[z.rhs :] + low

    count = end - first
    groups = count // STEP

    def body(i, carry):
        group(first + i * STEP, STEP)
        return carry

    lax.fori_loop(0, groups, body, 0)
    at = first + groups * STEP
    size = STEP // 2
    while size:
        rest = count & size

        @pl.when(rest != 0)
        def _(at=at, size=size):
            group(at, size)

        at = at + rest
        size //= 2


def near_bounds(bounds_ref):
    here, away = bounds_ref[0], bounds_ref[1]
    total = here + away
    first = jnp.minimum(here, (total * NEAR_SHARES[0] // 16) // STEP * STEP)
    second = jnp.minimum(here, (total * NEAR_SHARES[1] // 16) // STEP * STEP)
    third = jnp.clip((total * NEAR_SHARES[2] // 16) - here, 0, away)
    return here, away, first, second, third


def near_kernel(z, part, items_ref, halo_ref, bounds_ref, tgt, src, val, *rest):
    here, away, first, second, third = near_bounds(bounds_ref)
    _, acc = rest[-2:]
    begin, end = ((0, first), (first, second), (second, here), (here, here))[part]
    if part < 3:
        run_items(z, items_ref, z.leaves, begin, end, src, tgt, val, acc)
    if part >= 2:
        begin, end = ((0, third), (third, away))[part - 2]
        run_items(z, halo_ref, 2 * z.half, begin, end, rest[0], tgt, rest[1], acc)


def packed(blocks):
    return blocks[0] if len(blocks) == 1 else jnp.concatenate(blocks, axis=1)


def couple(kernel_high, kernel_low, high, low):
    rows = high.shape[0]
    both = dot(jnp.concatenate([high, low], axis=0), kernel_high, 1, 1)
    return both[:rows] + both[rows:] + dot(high, kernel_low, 1, 1)


def local_kernel(z, bounds_ref, slots_ref, own_ref, a_ref, b_ref, out_ref, feats, vals, rows_ref):
    parity = bounds_ref[2] % 2
    rank = z.rank
    start, width = z.message_c[0], z.message_term - z.message_c[0]
    a, b = a_ref[:, start : start + width], b_ref[:, start : start + width]
    sides = [jnp.where(parity == 0, b, a), jnp.where(parity == 0, a, b)]
    own = own_ref[...]
    blank_features = jnp.zeros((FEATURES, rank), bf16)
    blank_values = jnp.zeros((2 * z.rhs, rank), bf16)

    def store(at, features, values):
        feats[0, at] = jnp.concatenate([features, blank_features], axis=1)
        feats[1, at] = jnp.concatenate([blank_features, features], axis=1)
        vals[0, at] = jnp.concatenate([values, blank_values], axis=1)
        vals[1, at] = jnp.concatenate([blank_values, values], axis=1)

    def prepared(block):
        high, low = split2(block[: z.rhs] * GAIN)
        return (
            source_features(block[z.rhs :]).astype(bf16),
            jnp.concatenate([high, low], axis=0),
        )

    side_tables = [prepared(side) for side in sides]
    own_features, own_values = prepared(own)
    vals[0, z.ext_nodes] = jnp.zeros((2 * z.rhs, 2 * rank), bf16)
    vals[1, z.ext_nodes] = jnp.zeros((2 * z.rhs, 2 * rank), bf16)
    for level in range(z.levels):
        count, half, base = z.counts[level], halves(z.counts[level]), z.ext_offsets[level]
        for i in range(half):
            at = z.message_c[level] - start + i * rank
            for (features, values), first in zip(side_tables, (base, base + half + count)):
                store(first + i, features[:, at : at + rank], values[:, at : at + rank])
        for i in range(count):
            at = (z.offsets[level] + i) * rank
            store(base + half + i, own_features[:, at : at + rank], own_values[:, at : at + rank])
    target = target_features(own[z.rhs :])
    for at in range(0, z.packed, 2 * rank):
        turned = target[:, at : at + 2 * rank].T.astype(bf16)
        rows_ref[at : at + 2 * rank] = turned
    for node in range(z.nodes):
        used = bounds_ref[3 + node]
        points, values = [], []
        for slot in range(0, z.slots, 2):
            at = [slots_ref[node * z.slots + slot + k] for k in range(2)]
            points.append(feats[0, at[0]] + feats[1, at[1]])
            at = [jnp.where(slot + k < used, at[k], z.ext_nodes) for k in range(2)]
            values.append(vals[0, at[0]] + vals[1, at[1]])
        rows = rows_ref[node * rank : (node + 1) * rank]
        high, low = split2(kernel_of(dot(rows, packed(points), 1, 0)))
        values = packed(values)
        both = dot(values, high, 1, 1)
        out_ref[node] = both[: z.rhs] + both[z.rhs :] + dot(values[: z.rhs], low, 1, 1)


def upper_kernels(z, k, level, device, upper_ref, skel_ref):
    anchor = z.anchor(device, level)
    target = target_features(pad8(skel_ref[:, anchor, :])).T.astype(bf16)
    points = []
    for slot in range(z.level_slots(level)):
        source = upper_ref[k * z.slots + slot]
        points.append(pad8(skel_ref[:, jnp.where(source < 0, anchor, source), :]))
    return split2(kernel_of(dot(target, source_features(packed(points)).astype(bf16), 1, 0)))


def upper_sources(z, k, level, device, upper_ref, table):
    anchor = z.anchor(device, level)
    coefs = []
    for slot in range(z.level_slots(level)):
        source = upper_ref[k * z.slots + slot]
        coefs.append(table(jnp.where(source < 0, 0, source ^ anchor)) * jnp.where(source < 0, 0.0, GAIN))
    return split2(packed(coefs))


def upper_widths(z):
    return [z.level_slots(level) * z.rank for level in z.upper_levels if level <= z.top and z.level_slots(level)]


def top_kernel(z, bounds_ref, upper_ref, skel_ref, *outs):
    device = bounds_ref[2]
    at = 0
    for k, level in enumerate(z.upper_levels):
        if level <= z.top and z.level_slots(level):
            outs[at][...], outs[at + 1][...] = upper_kernels(z, k, level, device, upper_ref, skel_ref)
            at += 2


def mid_kernel(z, bounds_ref, upper_ref, fields_ref, basis_ref, transfer_ref, skel_ref, matrix_ref, *rest):
    tables = rest[: z.depth - 1 - z.top]
    _, acc, weights = rest[-3:]
    device = bounds_ref[2]
    rank, rhs = z.rank, z.rhs
    row = lax.broadcasted_iota(jnp.int32, (rhs + rank, rank), 0)
    column = lax.broadcasted_iota(jnp.int32, (rhs + rank, rank), 1)
    path = jnp.where(row - rhs == column, 1.0, 0.0)
    none = jnp.zeros((rank, rank), f32)
    for k, level in enumerate(z.upper_levels):
        if level <= z.top:
            continue
        table = tables[z.depth - 1 - level]
        path = matmul(path, matrix_ref[z.anchor(device, level)], 1, 1)
        if z.level_slots(level):
            kernel_high, kernel_low = upper_kernels(z, k, level, device, upper_ref, skel_ref)
            high, low = upper_sources(z, k, level, device, upper_ref, lambda at: table[at])
            field = couple(kernel_high, kernel_low, high, low)
            path = path + jnp.concatenate([field, none], axis=0)
    path = matmul(path, transfer_ref[z.nodes - 1], 1, 1)
    paths = [path + jnp.concatenate([fields_ref[z.nodes - 1], none], axis=0)]
    for level in range(z.levels - 2, -1, -1):
        below = []
        for i, path in enumerate(paths):
            node = z.offsets[level] + 2 * i
            both = matmul(path, transfer_ref[node : node + 2].reshape(2 * rank, rank), 1, 1)
            for child in range(2):
                lower = both[:, child * rank : (child + 1) * rank]
                below.append(lower + jnp.concatenate([fields_ref[node + child], none], axis=0))
        paths = below
    for leaf in range(z.leaves):
        values = matmul(paths[leaf], basis_ref[leaf])
        acc[leaf] += values[:rhs]
        high, low = split2(values[rhs:])
        weights[0, leaf] = high
        weights[1, leaf] = low


def final_kernel(z, bounds_ref, upper_ref, acc, weights, matrix_ref, *rest):
    out_ref, rest = rest[-1], rest[:-1]
    pieces, kernels = rest[: z.top + 1], rest[z.top + 1 :]
    device = bounds_ref[2]
    current = [piece[j] for piece in pieces for j in range(piece.shape[0])]
    values = {z.top: current}
    for level in range(z.top, 1, -1):
        anchor = z.anchor(device, level)
        moved = [matmul(current[j], matrix_ref[anchor ^ j]) for j in range(len(current))]
        current = [moved[2 * j] + moved[2 * j + 1] for j in range(len(current) // 2)]
        values[level - 1] = current
    downward, at = None, 0
    for k, level in enumerate(z.upper_levels):
        if level > z.top:
            continue
        if z.level_slots(level):

            def table(place, level=level):
                chosen = jnp.zeros((z.rhs, z.rank), f32)
                for j in range(1, len(values[level])):
                    chosen = jnp.where(place == j, values[level][j], chosen)
                return chosen

            high, low = upper_sources(z, k, level, device, upper_ref, table)
            field = couple(kernels[at][...], kernels[at + 1][...], high, low)
            at += 2
        else:
            field = jnp.zeros((z.rhs, z.rank), f32)
        if downward is None:
            downward = field
        else:
            downward = field + matmul(downward, matrix_ref[z.anchor(device, level)], 1, 1)
    high, low = split2(downward)
    stacked = jnp.concatenate([high, low], axis=0)
    for leaf in range(z.leaves):
        both = dot(stacked, weights[0, leaf], 1, 0)
        value = both[: z.rhs] + both[z.rhs :] + dot(high, weights[1, leaf], 1, 0)
        out_ref[:, leaf * z.leaf : (leaf + 1) * z.leaf] = acc[leaf] + value


SMEM = pl.BlockSpec(memory_space=pltpu.SMEM)
VMEM = pl.BlockSpec(memory_space=pltpu.VMEM)


def on_chip(x):
    return pltpu.with_memory_space_constraint(x, pltpu.VMEM)


def scalars(x):
    return pltpu.with_memory_space_constraint(x, pltpu.SMEM)


def call(body, outs, smem, vmem, scratch=(), aliases=None, cost=1.0, in_hbm=False, out_hbm=False):
    many = isinstance(outs, (list, tuple))
    listed = list(outs) if many else [outs]
    specs = [SMEM if o.dtype == jnp.int32 else VMEM for o in listed]
    shapes = [
        jax.ShapeDtypeStruct(o.shape, o.dtype)
        if out_hbm
        else (pltpu.SMEM if o.dtype == jnp.int32 else pltpu.VMEM)(o.shape, o.dtype)
        for o in listed
    ]
    if not in_hbm:
        smem, vmem = map(scalars, smem), map(on_chip, vmem)
    smem, vmem = list(smem), list(vmem)
    return pl.pallas_call(
        body,
        out_shape=shapes if many else shapes[0],
        in_specs=[SMEM] * len(smem) + [VMEM] * len(vmem),
        out_specs=specs if many else specs[0],
        scratch_shapes=list(scratch),
        input_output_aliases=aliases or {},
        compiler_params=pltpu.CompilerParams(vmem_limit_bytes=16 << 20),
        cost_estimate=pl.CostEstimate(
            flops=int(cost * 1e8), bytes_accessed=int(cost * 3e6), transcendentals=0
        ),
    )(*smem, *vmem)


def flip(x, axis, bit):
    return lax.ppermute(x, axis, [(i, i ^ bit) for i in range(lax.axis_size(axis))])


def shape(*dims, dtype=f32):
    return jax.ShapeDtypeStruct(dims, dtype)


def on_device(
    right_sides,
    points,
    basis,
    transfer,
    skeleton,
    near_list,
    near_count,
    inter_list,
    inter_count,
    upper_transfer,
    upper_skeleton,
    upper_list,
    upper_count,
):
    z = Sizes(
        lax.axis_size("group"),
        lax.axis_size("bulk"),
        basis.shape[0],
        basis.shape[1],
        basis.shape[2],
        right_sides.shape[0],
        near_list.shape[1],
        inter_list.shape[1],
    )
    part = functools.partial
    integers = part(shape, dtype=jnp.int32)
    halfs = part(shape, dtype=bf16)
    info = lax.axis_index(AXES).astype(jnp.int32).reshape(1)
    skeleton, upper_skeleton = skeleton.transpose(1, 0, 2), upper_skeleton.transpose(1, 0, 2)
    message = shape(z.rhs + 8, z.message)

    to_partner, to_other, own, term, items, halo_items, bounds, slots, upper = call(
        part(up_kernel, z),
        [
            message,
            message,
            shape(z.rhs + 8, z.packed),
            shape(z.rhs, z.rank),
            integers(z.leaves * (z.near + 1) + 1),
            integers(z.leaves * z.near + 1),
            integers(3 + z.nodes),
            integers(z.nodes * z.slots),
            integers(len(z.upper_levels) * z.slots),
        ],
        [info, near_list, near_count, inter_list.T, inter_count, upper_list.T, upper_count],
        [right_sides, points, basis, transfer, skeleton],
        cost=2.0,
        in_hbm=True,
    )
    from_partner = flip(to_partner, "bulk", 1)
    sources = (2 * z.rhs, z.leaf)
    src, tgt, val, acc = call(
        part(own_kernel, z),
        [
            halfs(z.leaves, z.leaf, FEATURES),
            halfs(z.leaves, FEATURES, z.leaf),
            halfs(z.leaves, *sources),
            shape(z.leaves, z.rhs, z.leaf),
        ],
        [],
        [right_sides, points],
        cost=0.7,
    )
    terms = call(
        part(pair_kernel, z),
        shape(z.depth - z.top, z.rhs, z.rank),
        [bounds],
        [term, from_partner, upper_transfer],
        cost=0.3,
    )
    pairs = [(i, i + 1) for i in range(1, z.devices - 1, 2)]
    from_other = lax.ppermute(to_other, AXES, pairs + [(b, a) for a, b in pairs])

    whole_levels, partial = [], terms
    for bit in range(1, z.bulk.bit_length()):
        whole_levels.append([partial[:1]])
        partial = partial[1:]
        if bit == z.bulk.bit_length() - 1:
            break
        sizes = [sum(p.shape[0] for p in level) for level in whole_levels]
        sent = jnp.concatenate([p for level in whole_levels for p in level] + [partial], axis=0)
        received = flip(sent, "bulk", 1 << bit)
        at = 0
        for level, size in zip(whole_levels, sizes):
            level.append(received[at : at + size])
            at += size
        partial = partial + received[at:]
    top = whole_levels.pop()
    whole_levels = [jnp.concatenate(level, axis=0) for level in whole_levels]
    for bit in range(z.top):
        top.append(flip(jnp.concatenate(top, axis=0), "group", 1 << bit))

    def near(index, acc, more=()):
        arrays = [tgt, src, val, *more, acc]
        return call(
            part(near_kernel, z, index),
            shape(z.leaves, z.rhs, z.leaf),
            [items, halo_items, bounds],
            arrays,
            aliases={2 + len(arrays): 0},
            cost=2.0,
        )

    acc = near(0, acc)
    acc = near(1, acc)
    halo_tables = call(
        part(halo_kernel, z),
        [halfs(2 * z.half, z.leaf, FEATURES), halfs(2 * z.half, *sources)],
        [bounds],
        [from_partner, from_other],
        cost=0.5,
    )
    acc = near(2, acc, halo_tables)
    acc = near(3, acc, halo_tables)
    fields = call(
        part(local_kernel, z),
        shape(z.nodes, z.rhs, z.rank),
        [bounds, slots],
        [own, from_partner, from_other],
        scratch=[
            pltpu.VMEM((2, z.ext_nodes, FEATURES, 2 * z.rank), bf16),
            pltpu.VMEM((2, z.ext_nodes + 1, 2 * z.rhs, 2 * z.rank), bf16),
            pltpu.VMEM((z.packed, FEATURES), bf16),
        ],
        cost=1.5,
    )
    kernels = call(
        part(top_kernel, z),
        [halfs(z.rank, width) for width in upper_widths(z) for _ in range(2)],
        [bounds, upper],
        [upper_skeleton],
        cost=0.3,
    )
    acc, weights = call(
        part(mid_kernel, z),
        [shape(z.leaves, z.rhs, z.leaf), halfs(2, z.leaves, z.rank, z.leaf)],
        [bounds, upper],
        [fields, basis, transfer, upper_skeleton, upper_transfer, *whole_levels, acc],
        aliases={7 + len(whole_levels): 0},
        cost=1.0,
    )
    return call(
        part(final_kernel, z),
        shape(*right_sides.shape),
        [bounds, upper],
        [acc, weights, upper_transfer, *top, *kernels],
        cost=1.0,
        out_hbm=True,
    )


def solution(mesh):
    in_specs = (
        P(None, AXES),
        P(None, AXES),
        P(AXES, None, None),
        P(AXES, None, None),
        P(AXES, None, None),
        P(AXES, None),
        P(AXES),
        P(AXES, None),
        P(AXES),
        P(),
        P(),
        P(),
        P(),
    )
    return jax.shard_map(
        on_device, mesh=mesh, in_specs=in_specs, out_specs=P(None, AXES), check_vma=False
    )
```

```python
import functools
import math

import jax
import jax.numpy as jnp
from jax import lax
from jax.experimental import pallas as pl
from jax.experimental.pallas import tpu as pltpu
from jax.sharding import PartitionSpec as P


AMPLITUDE = 0.2
KERNEL_RATE = 2.0
SOFTENING = 0.01
NUGGET = 0.5
SCALE = KERNEL_RATE * math.log2(math.e)
FLOOR = SOFTENING * SCALE * SCALE
SHIFT = 1.0 / math.log(2.0)
GAIN = AMPLITUDE * math.log(2.0)
FEATURES = 48
STEP = 4
NEAR_SHARES = (5, 10)
AXES = ("group", "bulk")

f32 = jnp.float32
bf16 = jnp.bfloat16


def dot(a, b, ca, cb):
    return lax.dot_general(a, b, (((ca,), (cb,)), ((), ())), preferred_element_type=f32)


def split2(x):
    high = x.astype(bf16)
    return high, (x - high.astype(f32)).astype(bf16)


def split3(x):
    a = x.astype(bf16).astype(f32)
    b = (x - a).astype(bf16).astype(f32)
    return a, b, x - a - b


def matmul(a, b, ca=1, cb=0):
    ah, al = split2(a)
    bh, bl = split2(b)
    rows = a.shape[1 - ca]
    if ca == 1:
        both = dot(jnp.concatenate([ah, al], axis=0), bh, ca, cb)
        return both[:rows] + both[rows:] + dot(ah, bl, ca, cb)
    return dot(ah, bh, ca, cb) + dot(al, bh, ca, cb) + dot(ah, bl, ca, cb)


def scaled_points(coords):
    u = coords * SCALE
    return u, jnp.broadcast_to(jnp.sum(u * u, axis=0, keepdims=True), u.shape)


def place(row, vector, first, second, third):
    rest = jnp.where(row == 5, third, 0.0)
    rest = jnp.where(row == 4, second, rest)
    rest = jnp.where(row == 3, first, rest)
    return jnp.where(row < 3, vector, rest)


def source_features(coords):
    u, length = scaled_points(coords)
    row = lax.broadcasted_iota(jnp.int32, u.shape, 0)
    a, b, c = split3(u)
    return jnp.concatenate(
        [place(row, a, *split3(length)), place(row, a, 1.0, 1.0, 1.0), b, b, a, c], axis=0
    )


def target_features(coords):
    u, length = scaled_points(coords)
    row = lax.broadcasted_iota(jnp.int32, u.shape, 0)
    a, b, c = split3(-2.0 * u)
    return jnp.concatenate(
        [place(row, a, 1.0, 1.0, 1.0), place(row, b, *split3(length + FLOOR)), a, b, c, a], axis=0
    )


def kernel_of(square):
    t = square * lax.rsqrt(square)
    return (SHIFT + t) * jnp.exp2(-t)


def halves(nodes):
    return max(nodes // 2, 1)


class Sizes:
    def __init__(self, mesh_group, mesh_bulk, leaves, rank, leaf, rhs, near, slots):
        self.group, self.bulk = mesh_group, mesh_bulk
        self.devices = mesh_group * mesh_bulk
        self.leaves, self.rank, self.leaf, self.rhs = leaves, rank, leaf, rhs
        self.near, self.slots = near, slots
        self.levels = leaves.bit_length()
        self.counts = [leaves >> level for level in range(self.levels)]
        self.offsets = [2 * leaves - 2 * count for count in self.counts]
        self.nodes = 2 * leaves - 1
        self.depth = self.devices.bit_length() - 1
        self.top = mesh_group.bit_length() - 1
        self.half = halves(leaves)
        assert 2 * self.half == leaves and leaves & (leaves - 1) == 0
        self.message_c = []
        at = self.half * leaf
        for count in self.counts:
            self.message_c.append(at)
            at += halves(count) * rank
        self.message_term = -(-at // 128) * 128
        self.message = self.message_term + -(-rank // 128) * 128
        self.packed = -(-self.nodes * rank // 128) * 128
        self.ext_counts = [count + 2 * halves(count) for count in self.counts]
        self.upper_levels = list(range(1, self.depth))

    def level_size(self, level):
        return self.bulk >> (self.depth - level) if level > self.top else 1 << level

    def level_slots(self, level):
        return min(self.slots, self.level_size(level) - 1)

    def anchor(self, device, level):
        return (self.devices + device) >> (self.depth - level)


def up_kernel(
    z, info_ref, near_list_in, near_count_in, upper_list_in, upper_count_in,
    rhs_in, pts_in, basis_in, transfer_in, skel_in, inter_list_in, inter_count_in, upper_skel_in,
    near_msg, far_msg, own_ref, term_ref, items_ref, halo_ref, bounds_ref, upper_ref,
    rhs_ref, pts_ref, basis_ref, transfer_ref, inter_list_ref, inter_count_ref, upper_skel_ref,
    skel_ref, near_list, near_count, upper_list, upper_count, sems,
):
    moves = (
        (near_list_in, near_list),
        (near_count_in, near_count),
        (upper_list_in, upper_list),
        (upper_count_in, upper_count),
        (rhs_in, rhs_ref),
        (basis_in, basis_ref),
        (transfer_in, transfer_ref),
        (skel_in, skel_ref),
        (pts_in, pts_ref),
        (inter_list_in, inter_list_ref),
        (inter_count_in, inter_count_ref),
        (upper_skel_in, upper_skel_ref),
    )
    copies = [pltpu.make_async_copy(*move, sems.at[i]) for i, move in enumerate(moves)]
    for copy in copies:
        copy.start()
    for copy in copies[:4]:
        copy.wait()
    device = info_ref[0]
    parity = device % 2
    for leaf in range(z.leaves):
        items_ref[leaf] = leaf * (z.leaves + 1)
    here = jnp.int32(z.leaves)
    away = jnp.int32(0)
    base = device * z.leaves
    for leaf in range(z.leaves):
        count = near_count[leaf]
        for slot in range(z.near):
            source = near_list[leaf, slot] - base
            used = (slot < count).astype(jnp.int32)
            inside = jnp.where(source // z.leaves == 0, used, 0)
            items_ref[here] = source + leaf * z.leaves
            halo_ref[away] = jnp.bitwise_and(source + z.half, 2 * z.half - 1) + leaf * 2 * z.half
            here = here + inside
            away = away + used - inside
    bounds_ref[0] = here
    bounds_ref[1] = away
    bounds_ref[2] = device
    for k, level in enumerate(z.upper_levels):
        anchor = z.anchor(device, level)
        used = upper_count[anchor]
        for slot in range(z.level_slots(level)):
            upper_ref[k * z.slots + slot] = jnp.where(slot < used, upper_list[slot, anchor], -1)

    for copy in copies[4:]:
        copy.wait()
    pair = 2 * z.rank
    rows, spare = slice(0, z.rhs), slice(z.rhs, z.rhs + 8)
    coords = slice(z.rhs, z.rhs + 3)
    own_ref[spare, :] = jnp.zeros((8, z.packed), f32)
    for node in range(z.nodes):
        own_ref[coords, node * z.rank : (node + 1) * z.rank] = skel_ref[:, node, :]
    pieces = []
    for leaf in range(z.leaves):
        at = leaf * z.leaf
        pieces.append(matmul(rhs_ref[:, at : at + z.leaf], basis_ref[leaf], 1, 1))
    for level in range(z.levels):
        first = z.offsets[level]
        if len(pieces) == 1:
            own_ref[rows, first * z.rank : (first + 1) * z.rank] = pieces[0]
            break
        raised = []
        for i in range(len(pieces) // 2):
            both = jnp.concatenate([pieces[2 * i], pieces[2 * i + 1]], axis=1)
            node = first + 2 * i
            own_ref[rows, node * z.rank : node * z.rank + pair] = both
            raised.append(matmul(both, transfer_ref[node : node + 2].reshape(pair, z.rank)))
        pieces = raised
    term = matmul(pieces[0], transfer_ref[z.nodes - 1])
    term_ref[...] = term
    width = z.half * z.leaf
    for ref, other in ((near_msg, 0), (far_msg, 1)):
        last = (parity + 1 + other) % 2
        at = pl.multiple_of(last * ((z.leaves - z.half) * z.leaf), 128)
        ref[spare, :] = jnp.zeros((8, z.message), f32)
        ref[rows, 0:width] = rhs_ref[:, pl.ds(at, width)]
        ref[coords, 0:width] = pts_ref[:, pl.ds(at, width)]
        for level in range(z.levels):
            size = halves(z.counts[level]) * z.rank
            first = z.offsets[level] * z.rank
            shift = (z.counts[level] - halves(z.counts[level])) * z.rank
            here = slice(z.message_c[level], z.message_c[level] + size)
            low = own_ref[:, first : first + size]
            if shift:
                low = jnp.where(last == 1, own_ref[:, first + shift : first + shift + size], low)
            ref[:, here] = low
        ref[rows, z.message_term : z.message_term + z.rank] = term


def pair_kernel(z, bounds_ref, term_ref, a_ref, matrix_ref, out_ref):
    device = bounds_ref[2]
    term = term_ref[...] + a_ref[0 : z.rhs, z.message_term : z.message_term + z.rank]
    out_ref[0] = term
    for i, level in enumerate(range(z.depth - 1, z.top, -1)):
        term = matmul(term, matrix_ref[z.anchor(device, level)])
        out_ref[i + 1] = term


def pad8(block):
    return jnp.concatenate([block, jnp.zeros((8 - block.shape[0], block.shape[1]), f32)], axis=0)


def fill_sources(z, src, val, first, values, coords):
    high, low = split2(values * GAIN)
    features = source_features(coords)
    for i in range(values.shape[1] // z.leaf):
        here = slice(i * z.leaf, (i + 1) * z.leaf)
        val[first + i, 0 : z.rhs] = high[:, here]
        val[first + i, z.rhs : 2 * z.rhs] = low[:, here]
        src[first + i] = features[:, here].T.astype(bf16)


def own_kernel(z, rhs_ref, pts_ref, src, tgt, val, acc):
    coords = pad8(pts_ref[...])
    fill_sources(z, src, val, 0, rhs_ref[...], coords)
    features = target_features(coords).astype(bf16)
    for i in range(z.leaves):
        here = slice(i * z.leaf, (i + 1) * z.leaf)
        tgt[i] = features[:, here]
        acc[i] = NUGGET * rhs_ref[:, here]


def halo_kernel(z, bounds_ref, a_ref, b_ref, src, val):
    width = z.half * z.leaf
    parity = bounds_ref[2] % 2
    left = jnp.where(parity == 0, b_ref[:, 0:width], a_ref[:, 0:width])
    right = jnp.where(parity == 0, a_ref[:, 0:width], b_ref[:, 0:width])
    fill_sources(z, src, val, 0, left[0 : z.rhs], left[z.rhs : z.rhs + 8])
    fill_sources(z, src, val, z.half, right[0 : z.rhs], right[z.rhs : z.rhs + 8])


def run_items(z, list_ref, per_target, first, end, src, tgt, val, acc):
    def group(at, size):
        for k in range(size):
            item = list_ref[at + k]
            target, source = item // per_target, item % per_target
            kernel_high, kernel_low = split2(kernel_of(dot(src[source], tgt[target], 1, 0)))
            values = val[source]
            both = dot(values, kernel_high, 1, 0)
            low = dot(values[: z.rhs], kernel_low, 1, 0)
            acc[target] += both[: z.rhs] + both[z.rhs :] + low

    count = end - first
    groups = count // STEP

    def body(i, carry):
        group(first + i * STEP, STEP)
        return carry

    lax.fori_loop(0, groups, body, 0)
    at = first + groups * STEP
    size = STEP // 2
    while size:
        rest = count & size

        @pl.when(rest != 0)
        def _(at=at, size=size):
            group(at, size)

        at = at + rest
        size //= 2


def near_kernel(z, part, items_ref, halo_ref, bounds_ref, tgt, src, val, *rest):
    here, away = bounds_ref[0], bounds_ref[1]
    cuts = [jnp.minimum(here, (here + away) * share // 16 // STEP * STEP) for share in NEAR_SHARES]
    begin, end = ((0, cuts[0]), (cuts[0], cuts[1]), (cuts[1], here))[part]
    acc = rest[-1]
    run_items(z, items_ref, z.leaves, begin, end, src, tgt, val, acc)
    if part == 2:
        run_items(z, halo_ref, 2 * z.half, 0, away, rest[0], tgt, rest[1], acc)


def packed(blocks):
    return blocks[0] if len(blocks) == 1 else jnp.concatenate(blocks, axis=1)


def couple(kernel_high, kernel_low, high, low):
    rows = high.shape[0]
    both = dot(jnp.concatenate([high, low], axis=0), kernel_high, 1, 1)
    return both[:rows] + both[rows:] + dot(high, kernel_low, 1, 1)


def local_kernel(z, bounds_ref, list_ref, count_ref, own_ref, a_ref, b_ref, out_ref):
    device = bounds_ref[2]
    parity = device % 2
    rank = z.rank
    start, width = z.message_c[0], z.message_term - z.message_c[0]
    a, b = a_ref[:, start : start + width], b_ref[:, start : start + width]
    sides = [jnp.where(parity == 0, b, a), jnp.where(parity == 0, a, b)]
    own = own_ref[...]

    def prepared(block):
        high, low = split2(block[: z.rhs] * GAIN)
        features = source_features(block[z.rhs :]).astype(bf16)
        return features, jnp.concatenate([high, low], axis=0)

    left, right = [prepared(side) for side in sides]
    middle = prepared(own)
    target = target_features(own[z.rhs :])
    slot = lax.broadcasted_iota(jnp.int32, (z.slots, z.nodes), 0)
    sources = jnp.where(slot < count_ref[...], list_ref[...], -1).T
    for level in range(z.levels):
        count, half, first = z.counts[level], halves(z.counts[level]), z.offsets[level]
        at = z.message_c[level] - start
        features, values = [
            jnp.concatenate(
                [
                    left[k][:, at : at + half * rank],
                    middle[k][:, first * rank : (first + count) * rank],
                    right[k][:, at : at + half * rank],
                ],
                axis=1,
            )
            for k in range(2)
        ]
        total = z.ext_counts[level]
        here = lax.broadcasted_iota(jnp.int32, (count, total * rank), 1) // rank + device * count - half
        mask = jnp.zeros((count, total * rank), f32)
        for k in range(z.slots):
            mask = jnp.where(sources[first : first + count, k : k + 1] == here, 1.0, mask)
        mask = mask.astype(bf16)
        step = min(2, count)
        for i in range(0, count, step):
            low, high = i * rank, (i + step + 2 * half) * rank
            rows = target[:, (first + i) * rank : (first + i + step) * rank].T.astype(bf16)
            kernel_high, kernel_low = split2(kernel_of(dot(rows, features[:, low:high], 1, 0)))
            for k in range(step):
                chosen = values[:, low:high] * mask[i + k : i + k + 1, low:high]
                part = slice(k * rank, (k + 1) * rank)
                both = dot(chosen, kernel_high[part], 1, 1)
                low_part = dot(chosen[: z.rhs], kernel_low[part], 1, 1)
                out_ref[first + i + k] = both[: z.rhs] + both[z.rhs :] + low_part


def upper_kernels(z, k, level, device, upper_ref, skel_ref):
    anchor = z.anchor(device, level)
    target = target_features(pad8(skel_ref[:, anchor, :])).T.astype(bf16)
    points = []
    for slot in range(z.level_slots(level)):
        source = upper_ref[k * z.slots + slot]
        points.append(pad8(skel_ref[:, jnp.where(source < 0, anchor, source), :]))
    return split2(kernel_of(dot(target, source_features(packed(points)).astype(bf16), 1, 0)))


def upper_sources(z, k, level, device, upper_ref, table):
    anchor = z.anchor(device, level)
    coefs = []
    for slot in range(z.level_slots(level)):
        source = upper_ref[k * z.slots + slot]
        coefs.append(table(jnp.where(source < 0, 0, source ^ anchor)) * jnp.where(source < 0, 0.0, GAIN))
    return split2(packed(coefs))


def upper_widths(z):
    return [z.level_slots(level) * z.rank for level in z.upper_levels if level <= z.top and z.level_slots(level)]


def top_kernel(z, bounds_ref, upper_ref, skel_ref, *outs):
    device = bounds_ref[2]
    at = 0
    for k, level in enumerate(z.upper_levels):
        if level <= z.top and z.level_slots(level):
            outs[at][...], outs[at + 1][...] = upper_kernels(z, k, level, device, upper_ref, skel_ref)
            at += 2


def mid_kernel(z, bounds_ref, upper_ref, fields_ref, basis_ref, transfer_ref, skel_ref, matrix_ref, *rest):
    tables = rest[: z.depth - 1 - z.top]
    _, acc, weights = rest[-3:]
    device = bounds_ref[2]
    rank, rhs = z.rank, z.rhs
    row = lax.broadcasted_iota(jnp.int32, (rhs + rank, rank), 0)
    column = lax.broadcasted_iota(jnp.int32, (rhs + rank, rank), 1)
    path = jnp.where(row - rhs == column, 1.0, 0.0)
    none = jnp.zeros((rank, rank), f32)
    for k, level in enumerate(z.upper_levels):
        if level <= z.top:
            continue
        table = tables[z.depth - 1 - level]
        path = matmul(path, matrix_ref[z.anchor(device, level)], 1, 1)
        if z.level_slots(level):
            kernel_high, kernel_low = upper_kernels(z, k, level, device, upper_ref, skel_ref)
            high, low = upper_sources(z, k, level, device, upper_ref, lambda at: table[at])
            field = couple(kernel_high, kernel_low, high, low)
            path = path + jnp.concatenate([field, none], axis=0)
    path = matmul(path, transfer_ref[z.nodes - 1], 1, 1)
    paths = [path + jnp.concatenate([fields_ref[z.nodes - 1], none], axis=0)]
    for level in range(z.levels - 2, -1, -1):
        below = []
        for i, path in enumerate(paths):
            node = z.offsets[level] + 2 * i
            both = matmul(path, transfer_ref[node : node + 2].reshape(2 * rank, rank), 1, 1)
            for child in range(2):
                lower = both[:, child * rank : (child + 1) * rank]
                below.append(lower + jnp.concatenate([fields_ref[node + child], none], axis=0))
        paths = below
    for leaf in range(z.leaves):
        values = matmul(paths[leaf], basis_ref[leaf])
        acc[leaf] += values[:rhs]
        high, low = split2(values[rhs:])
        weights[0, leaf] = high
        weights[1, leaf] = low


def final_kernel(z, bounds_ref, upper_ref, acc, weights, matrix_ref, *rest):
    out_ref, rest = rest[-1], rest[:-1]
    pieces, kernels = rest[: z.top + 1], rest[z.top + 1 :]
    device = bounds_ref[2]
    current = [piece[j] for piece in pieces for j in range(piece.shape[0])]
    values = {z.top: current}
    for level in range(z.top, 1, -1):
        anchor = z.anchor(device, level)
        moved = [matmul(current[j], matrix_ref[anchor ^ j]) for j in range(len(current))]
        current = [moved[2 * j] + moved[2 * j + 1] for j in range(len(current) // 2)]
        values[level - 1] = current
    downward, at = None, 0
    for k, level in enumerate(z.upper_levels):
        if level > z.top:
            continue
        if z.level_slots(level):

            def table(place, level=level):
                chosen = jnp.zeros((z.rhs, z.rank), f32)
                for j in range(1, len(values[level])):
                    chosen = jnp.where(place == j, values[level][j], chosen)
                return chosen

            high, low = upper_sources(z, k, level, device, upper_ref, table)
            field = couple(kernels[at][...], kernels[at + 1][...], high, low)
            at += 2
        else:
            field = jnp.zeros((z.rhs, z.rank), f32)
        if downward is None:
            downward = field
        else:
            downward = field + matmul(downward, matrix_ref[z.anchor(device, level)], 1, 1)
    high, low = split2(downward)
    stacked = jnp.concatenate([high, low], axis=0)
    for leaf in range(z.leaves):
        both = dot(stacked, weights[0, leaf], 1, 0)
        value = both[: z.rhs] + both[z.rhs :] + dot(high, weights[1, leaf], 1, 0)
        out_ref[:, leaf * z.leaf : (leaf + 1) * z.leaf] = acc[leaf] + value


SMEM = pl.BlockSpec(memory_space=pltpu.SMEM)
VMEM = pl.BlockSpec(memory_space=pltpu.VMEM)


class Vector:
    def __init__(self, array):
        self.shape, self.dtype = array.shape, array.dtype


def call(body, outs, smem, vmem, scratch=(), aliases=None, cost=1.0, load=False, out_hbm=False):
    many = isinstance(outs, (list, tuple))
    listed = list(outs) if many else [outs]
    places = [
        pltpu.SMEM if o.dtype == jnp.int32 and not isinstance(o, Vector) else pltpu.VMEM for o in listed
    ]
    specs = [pl.BlockSpec(memory_space=place) for place in places]
    shapes = [
        jax.ShapeDtypeStruct(o.shape, o.dtype) if out_hbm else place(o.shape, o.dtype)
        for o, place in zip(listed, places)
    ]
    source = pltpu.HBM if load else pltpu.VMEM
    if not load:
        smem = [pltpu.with_memory_space_constraint(x, pltpu.SMEM) for x in smem]
    vmem = [pltpu.with_memory_space_constraint(x, source) for x in vmem]
    return pl.pallas_call(
        body,
        out_shape=shapes if many else shapes[0],
        in_specs=[SMEM] * len(smem) + [pl.BlockSpec(memory_space=source)] * len(vmem),
        out_specs=specs if many else specs[0],
        scratch_shapes=list(scratch),
        input_output_aliases=aliases or {},
        compiler_params=pltpu.CompilerParams(vmem_limit_bytes=16 << 20),
        cost_estimate=pl.CostEstimate(
            flops=int(cost * 1e8), bytes_accessed=int(cost * 3e6), transcendentals=0
        ),
    )(*smem, *vmem)


def flip(x, axis, bit):
    return lax.ppermute(x, axis, [(i, i ^ bit) for i in range(lax.axis_size(axis))])


def shape(*dims, dtype=f32):
    return jax.ShapeDtypeStruct(dims, dtype)


def on_device(
    right_sides,
    points,
    basis,
    transfer,
    skeleton,
    near_list,
    near_count,
    inter_list,
    inter_count,
    upper_transfer,
    upper_skeleton,
    upper_list,
    upper_count,
):
    z = Sizes(
        lax.axis_size("group"),
        lax.axis_size("bulk"),
        basis.shape[0],
        basis.shape[1],
        basis.shape[2],
        right_sides.shape[0],
        near_list.shape[1],
        inter_list.shape[1],
    )
    part = functools.partial
    integers = part(shape, dtype=jnp.int32)
    halfs = part(shape, dtype=bf16)
    info = lax.axis_index(AXES).astype(jnp.int32).reshape(1)
    skeleton, upper_skeleton = skeleton.transpose(1, 0, 2), upper_skeleton.transpose(1, 0, 2)
    inter_list, inter_count, upper_list = inter_list.T, inter_count.reshape(1, -1), upper_list.T
    message = shape(z.rhs + 8, z.message)

    to_partner, to_other, own, term, items, halo_items, bounds, upper, *kept = call(
        part(up_kernel, z),
        [
            message,
            message,
            shape(z.rhs + 8, z.packed),
            shape(z.rhs, z.rank),
            integers(z.leaves * (z.near + 1) + 1),
            integers(z.leaves * z.near + 1),
            integers(3),
            integers(len(z.upper_levels) * z.slots),
            *[shape(*a.shape, dtype=a.dtype) for a in (right_sides, points, basis, transfer)],
            *[Vector(a) for a in (inter_list, inter_count)],
            shape(*upper_skeleton.shape),
        ],
        [info],
        [near_list, near_count, upper_list, upper_count, right_sides, points, basis, transfer, skeleton, inter_list, inter_count, upper_skeleton],
        scratch=[
            pltpu.VMEM(skeleton.shape, f32),
            pltpu.SMEM(near_list.shape, jnp.int32),
            pltpu.SMEM(near_count.shape, jnp.int32),
            pltpu.SMEM(upper_list.shape, jnp.int32),
            pltpu.SMEM(upper_count.shape, jnp.int32),
            pltpu.SemaphoreType.DMA((12,)),
        ],
        cost=2.0,
        load=True,
    )
    right_sides, points, basis, transfer, inter_list, inter_count, upper_skeleton = kept
    from_partner = flip(to_partner, "bulk", 1)
    sources = (2 * z.rhs, z.leaf)
    src, tgt, val, acc = call(
        part(own_kernel, z),
        [
            halfs(z.leaves, z.leaf, FEATURES),
            halfs(z.leaves, FEATURES, z.leaf),
            halfs(z.leaves, *sources),
            shape(z.leaves, z.rhs, z.leaf),
        ],
        [],
        [right_sides, points],
        cost=0.7,
    )
    terms = call(
        part(pair_kernel, z),
        shape(z.depth - z.top, z.rhs, z.rank),
        [bounds],
        [term, from_partner, upper_transfer],
        cost=0.3,
    )
    pairs = [(i, i + 1) for i in range(1, z.devices - 1, 2)]
    from_other = lax.ppermute(to_other, AXES, pairs + [(b, a) for a, b in pairs])

    whole_levels, partial = [], terms
    for bit in range(1, z.bulk.bit_length()):
        whole_levels.append([partial[:1]])
        partial = partial[1:]
        if bit == z.bulk.bit_length() - 1:
            break
        sizes = [sum(p.shape[0] for p in level) for level in whole_levels]
        sent = jnp.concatenate([p for level in whole_levels for p in level] + [partial], axis=0)
        received = flip(sent, "bulk", 1 << bit)
        at = 0
        for level, size in zip(whole_levels, sizes):
            level.append(received[at : at + size])
            at += size
        partial = partial + received[at:]
    top = whole_levels.pop()
    whole_levels = [jnp.concatenate(level, axis=0) for level in whole_levels]
    for bit in range(z.top):
        top.append(flip(jnp.concatenate(top, axis=0), "group", 1 << bit))

    def near(index, acc, more=()):
        arrays = [tgt, src, val, *more, acc]
        return call(
            part(near_kernel, z, index),
            shape(z.leaves, z.rhs, z.leaf),
            [items, halo_items, bounds],
            arrays,
            aliases={2 + len(arrays): 0},
            cost=2.0,
        )

    acc = near(0, acc)
    acc = near(1, acc)
    halo_tables = call(
        part(halo_kernel, z),
        [halfs(2 * z.half, z.leaf, FEATURES), halfs(2 * z.half, *sources)],
        [bounds],
        [from_partner, from_other],
        cost=0.5,
    )
    acc = near(2, acc, halo_tables)
    fields = call(
        part(local_kernel, z),
        shape(z.nodes, z.rhs, z.rank),
        [bounds],
        [inter_list, inter_count, own, from_partner, from_other],
        cost=1.5,
    )
    kernels = call(
        part(top_kernel, z),
        [halfs(z.rank, width) for width in upper_widths(z) for _ in range(2)],
        [bounds, upper],
        [upper_skeleton],
        cost=0.3,
    )
    acc, weights = call(
        part(mid_kernel, z),
        [shape(z.leaves, z.rhs, z.leaf), halfs(2, z.leaves, z.rank, z.leaf)],
        [bounds, upper],
        [fields, basis, transfer, upper_skeleton, upper_transfer, *whole_levels, acc],
        aliases={7 + len(whole_levels): 0},
        cost=1.0,
    )
    return call(
        part(final_kernel, z),
        shape(*right_sides.shape),
        [bounds, upper],
        [acc, weights, upper_transfer, *top, *kernels],
        cost=1.0,
        out_hbm=True,
    )


def solution(mesh):
    in_specs = (
        P(None, AXES),
        P(None, AXES),
        P(AXES, None, None),
        P(AXES, None, None),
        P(AXES, None, None),
        P(AXES, None),
        P(AXES),
        P(AXES, None),
        P(AXES),
        P(),
        P(),
        P(),
        P(),
    )
    return jax.shard_map(
        on_device, mesh=mesh, in_specs=in_specs, out_specs=P(None, AXES), check_vma=False
    )
```

```python
import functools
import math

import jax
import jax.numpy as jnp
from jax import lax
from jax.experimental import pallas as pl
from jax.experimental.pallas import tpu as pltpu
from jax.sharding import PartitionSpec as P


AMPLITUDE = 0.2
KERNEL_RATE = 2.0
SOFTENING = 0.01
NUGGET = 0.5
SCALE = KERNEL_RATE * math.log2(math.e)
FLOOR = SOFTENING * SCALE * SCALE
SHIFT = 1.0 / math.log(2.0)
GAIN = AMPLITUDE * math.log(2.0)
FEATURES = 48
STEP = 8
NEAR_CUTS = (8, 24, 40)
AXES = ("group", "bulk")

f32 = jnp.float32
bf16 = jnp.bfloat16


def dot(a, b, ca, cb):
    return lax.dot_general(a, b, (((ca,), (cb,)), ((), ())), preferred_element_type=f32)


def split2(x):
    high = x.astype(bf16)
    return high, (x - high.astype(f32)).astype(bf16)


def split3(x):
    a = x.astype(bf16).astype(f32)
    b = (x - a).astype(bf16).astype(f32)
    return a, b, x - a - b


def matmul(a, b, ca=1, cb=0):
    ah, al = split2(a)
    bh, bl = split2(b)
    rows = a.shape[1 - ca]
    if ca == 1:
        both = dot(jnp.concatenate([ah, al], axis=0), bh, ca, cb)
        return both[:rows] + both[rows:] + dot(ah, bl, ca, cb)
    return dot(ah, bh, ca, cb) + dot(al, bh, ca, cb) + dot(ah, bl, ca, cb)


def scaled_points(coords):
    u = coords * SCALE
    return u, jnp.broadcast_to(jnp.sum(u * u, axis=0, keepdims=True), u.shape)


def place(row, vector, first, second, third):
    rest = jnp.where(row == 5, third, 0.0)
    rest = jnp.where(row == 4, second, rest)
    rest = jnp.where(row == 3, first, rest)
    return jnp.where(row < 3, vector, rest)


def source_features(coords):
    u, length = scaled_points(coords)
    row = lax.broadcasted_iota(jnp.int32, u.shape, 0)
    a, b, c = split3(u)
    return jnp.concatenate(
        [place(row, a, *split3(length)), place(row, a, 1.0, 1.0, 1.0), b, b, a, c], axis=0
    )


def target_features(coords):
    u, length = scaled_points(coords)
    row = lax.broadcasted_iota(jnp.int32, u.shape, 0)
    a, b, c = split3(-2.0 * u)
    return jnp.concatenate(
        [place(row, a, 1.0, 1.0, 1.0), place(row, b, *split3(length + FLOOR)), a, b, c, a], axis=0
    )


def kernel_of(square):
    t = square * lax.rsqrt(square)
    return (SHIFT + t) * jnp.exp2(-t)


def halves(nodes):
    return max(nodes // 2, 1)


class Sizes:
    def __init__(self, mesh_group, mesh_bulk, leaves, rank, leaf, rhs, near, slots):
        self.group, self.bulk = mesh_group, mesh_bulk
        self.devices = mesh_group * mesh_bulk
        self.leaves, self.rank, self.leaf, self.rhs = leaves, rank, leaf, rhs
        self.near, self.slots = near, slots
        self.levels = leaves.bit_length()
        self.counts = [leaves >> level for level in range(self.levels)]
        self.offsets = [2 * leaves - 2 * count for count in self.counts]
        self.nodes = 2 * leaves - 1
        self.depth = self.devices.bit_length() - 1
        self.top = mesh_group.bit_length() - 1
        self.half = halves(leaves)
        assert 2 * self.half == leaves and leaves & (leaves - 1) == 0
        self.message_c = []
        at = self.half * leaf
        for count in self.counts:
            self.message_c.append(at)
            at += halves(count) * rank
        self.message_term = -(-at // 128) * 128
        self.packed = -(-self.nodes * rank // 128) * 128
        self.ext_counts = [count + 2 * halves(count) for count in self.counts]
        self.upper_levels = list(range(1, self.depth))

    def level_size(self, level):
        return self.bulk >> (self.depth - level) if level > self.top else 1 << level

    def level_slots(self, level):
        return min(self.slots, self.level_size(level) - 1)

    @property
    def shared(self):
        return max(2 * self.group - 4, 0)

    def matrix(self, level):
        return self.shared + level - self.top - 1

    def place(self, device, level):
        return self.matrix(level) if level > self.top else self.anchor(device, level) - 4

    def anchor(self, device, level):
        return (self.devices + device) >> (self.depth - level)


def up_kernel(
    z, near_list_in, near_count_in, upper_list_in, upper_count_in,
    rhs_in, pts_in, basis_in, transfer_in, skel_in, inter_list_in, inter_count_in, upper_skel_in, matrix_in,
    near_msg, far_msg, own_ref, term_ref, where_ref, near_list, near_count, upper_list, upper_count,
    rhs_ref, pts_ref, basis_ref, transfer_ref, inter_list_ref, inter_count_ref, upper_skel_ref, matrix_ref,
    skel_ref, sems,
):
    device = lax.axis_index(AXES[0]) * z.bulk + lax.axis_index(AXES[1])
    moves = [
        (rhs_in, rhs_ref),
        (basis_in, basis_ref),
        (transfer_in, transfer_ref),
        (skel_in, skel_ref),
        (pts_in, pts_ref),
        (near_list_in, near_list),
        (near_count_in, near_count),
        (upper_list_in, upper_list),
        (upper_count_in, upper_count),
        (inter_list_in, inter_list_ref),
        (inter_count_in, inter_count_ref),
        (upper_skel_in, upper_skel_ref),
        (matrix_in.at[4 : 2 * z.group], matrix_ref.at[0 : z.shared]),
    ]
    for level in range(z.top + 1, z.depth):
        moves.append((matrix_in.at[z.anchor(device, level)], matrix_ref.at[z.matrix(level)]))
    copies = [pltpu.make_async_copy(*move, sems.at[i]) for i, move in enumerate(moves)]
    for copy in copies:
        copy.start()
    where_ref[0] = device
    parity = device % 2
    for copy in copies[:2]:
        copy.wait()
    pair = 2 * z.rank
    rows, spare = slice(0, z.rhs), slice(z.rhs, z.rhs + 8)
    coords = slice(z.rhs, z.rhs + 3)
    pieces = []
    for leaf in range(z.leaves):
        at = leaf * z.leaf
        pieces.append(matmul(rhs_ref[:, at : at + z.leaf], basis_ref[leaf], 1, 1))
    for copy in copies[2:]:
        copy.wait()
    own_ref[spare, :] = jnp.zeros((8, z.packed), f32)
    for node in range(z.nodes):
        own_ref[coords, node * z.rank : (node + 1) * z.rank] = skel_ref[:, node, :]
    for level in range(z.levels):
        first = z.offsets[level]
        if len(pieces) == 1:
            own_ref[rows, first * z.rank : (first + 1) * z.rank] = pieces[0]
            break
        raised = []
        for i in range(len(pieces) // 2):
            both = jnp.concatenate([pieces[2 * i], pieces[2 * i + 1]], axis=1)
            node = first + 2 * i
            own_ref[rows, node * z.rank : node * z.rank + pair] = both
            raised.append(matmul(both, transfer_ref[node : node + 2].reshape(pair, z.rank)))
        pieces = raised
    term = matmul(pieces[0], transfer_ref[z.nodes - 1])
    term_ref[...] = term
    width = z.half * z.leaf
    for ref, other in ((near_msg, 0), (far_msg, 1)):
        last = (parity + 1 + other) % 2
        at = pl.multiple_of(last * ((z.leaves - z.half) * z.leaf), 128)
        ref[spare, :] = jnp.zeros((8, ref.shape[1]), f32)
        ref[rows, 0:width] = rhs_ref[:, pl.ds(at, width)]
        ref[coords, 0:width] = pts_ref[:, pl.ds(at, width)]
        for level in range(z.levels):
            size = halves(z.counts[level]) * z.rank
            first = z.offsets[level] * z.rank
            shift = (z.counts[level] - halves(z.counts[level])) * z.rank
            here = slice(z.message_c[level], z.message_c[level] + size)
            low = own_ref[:, first : first + size]
            if shift:
                low = jnp.where(last == 1, own_ref[:, first + shift : first + shift + size], low)
            ref[:, here] = low


def lists_kernel(z, where_ref, near_list, near_count, upper_list, upper_count, items_ref, halo_ref, bounds_ref, upper_ref):
    device = where_ref[0]
    for leaf in range(z.leaves):
        items_ref[leaf] = leaf * (z.leaves + 1)
    here = jnp.int32(z.leaves)
    away = jnp.int32(0)
    base = device * z.leaves
    bits = z.leaves.bit_length() - 1
    for leaf in range(z.leaves):
        count = near_count[leaf]
        for slot in range(z.near):
            source = near_list[leaf, slot] - base
            used = (slot < count).astype(jnp.int32)
            inside = jnp.where(lax.shift_right_arithmetic(source, bits) == 0, used, 0)
            items_ref[here] = source + leaf * z.leaves
            halo_ref[away] = jnp.bitwise_and(source + z.half, 2 * z.half - 1) + leaf * 2 * z.half
            here = here + inside
            away = away + used - inside
    bounds_ref[0] = here
    bounds_ref[1] = away
    bounds_ref[2] = device
    for k, level in enumerate(z.upper_levels):
        anchor = z.anchor(device, level)
        used = upper_count[anchor]
        for slot in range(z.level_slots(level)):
            upper_ref[k * z.slots + slot] = jnp.where(slot < used, upper_list[slot, anchor], -1)


def pair_kernel(z, where_ref, term_ref, a_ref, matrix_ref, out_ref):
    term = term_ref[...] + a_ref[...]
    out_ref[0] = term
    for i, level in enumerate(range(z.depth - 1, z.top, -1)):
        term = matmul(term, matrix_ref[z.matrix(level)])
        out_ref[i + 1] = term


def pad8(block):
    return jnp.concatenate([block, jnp.zeros((8 - block.shape[0], block.shape[1]), f32)], axis=0)


def fill_sources(z, src, val, first, values, coords):
    high, low = split2(values * GAIN)
    features = source_features(coords)
    for i in range(values.shape[1] // z.leaf):
        here = slice(i * z.leaf, (i + 1) * z.leaf)
        val[first + i, 0 : z.rhs] = high[:, here]
        val[first + i, z.rhs : 2 * z.rhs] = low[:, here]
        src[first + i] = features[:, here].T.astype(bf16)


def own_kernel(z, rhs_ref, pts_ref, src, tgt, val, acc):
    coords = pad8(pts_ref[...])
    fill_sources(z, src, val, 0, rhs_ref[...], coords)
    features = target_features(coords).astype(bf16)
    for i in range(z.leaves):
        here = slice(i * z.leaf, (i + 1) * z.leaf)
        tgt[i] = features[:, here]
        acc[i] = NUGGET * rhs_ref[:, here]


def halo_kernel(z, bounds_ref, a_ref, b_ref, src, val):
    width = z.half * z.leaf
    parity = bounds_ref[2] % 2
    left = jnp.where(parity == 0, b_ref[:, 0:width], a_ref[:, 0:width])
    right = jnp.where(parity == 0, a_ref[:, 0:width], b_ref[:, 0:width])
    fill_sources(z, src, val, 0, left[0 : z.rhs], left[z.rhs : z.rhs + 8])
    fill_sources(z, src, val, z.half, right[0 : z.rhs], right[z.rhs : z.rhs + 8])


def run_items(z, list_ref, per_target, first, end, src, tgt, val, acc):
    bits = per_target.bit_length() - 1

    def load(at, size):
        items = [list_ref[at + k] for k in range(size)]
        targets = [lax.shift_right_logical(item, bits) for item in items]
        return targets, [jnp.bitwise_and(item, per_target - 1) for item in items]

    def group(targets, sources):
        for target, source in zip(targets, sources):
            kernel_high, kernel_low = split2(kernel_of(dot(src[source], tgt[target], 1, 0)))
            values = val[source]
            both = dot(values, kernel_high, 1, 0)
            low = dot(values[: z.rhs], kernel_low, 1, 0)
            acc[target] += both[: z.rhs] + both[z.rhs :] + low

    count = end - first
    groups = lax.shift_right_logical(count, STEP.bit_length() - 1)

    def body(i, ready):
        later = load(first + (i + 1) * STEP, STEP)
        group(*ready)
        return later

    lax.fori_loop(0, groups, body, load(first, STEP))
    at = first + groups * STEP
    size = STEP // 2
    while size:
        rest = jnp.bitwise_and(count, size)

        @pl.when(rest != 0)
        def _(at=at, size=size):
            group(*load(at, size))

        at = at + rest
        size //= 2


def near_kernel(z, part, items_ref, halo_ref, bounds_ref, tgt, src, val, *rest):
    here, away = bounds_ref[0], bounds_ref[1]
    cuts = [0] + [jnp.minimum(here, cut) for cut in NEAR_CUTS] + [here]
    begin, end = cuts[part], cuts[part + 1]
    acc = rest[-1]
    run_items(z, items_ref, z.leaves, begin, end, src, tgt, val, acc)
    if part == len(NEAR_CUTS):
        run_items(z, halo_ref, 2 * z.half, 0, away, rest[0], tgt, rest[1], acc)


def packed(blocks):
    return blocks[0] if len(blocks) == 1 else jnp.concatenate(blocks, axis=1)


def couple(kernel_high, kernel_low, high, low):
    rows = high.shape[0]
    both = dot(jnp.concatenate([high, low], axis=0), kernel_high, 1, 1)
    return both[:rows] + both[rows:] + dot(high, kernel_low, 1, 1)


def local_kernel(z, bounds_ref, list_ref, count_ref, own_ref, a_ref, b_ref, out_ref):
    device = bounds_ref[2]
    parity = device % 2
    rank = z.rank
    start, width = z.message_c[0], z.message_term - z.message_c[0]
    a, b = a_ref[:, start : start + width], b_ref[:, start : start + width]
    sides = [jnp.where(parity == 0, b, a), jnp.where(parity == 0, a, b)]
    own = own_ref[...]

    def prepared(block):
        high, low = split2(block[: z.rhs] * GAIN)
        return source_features(block[z.rhs :]), jnp.concatenate([high, low], axis=0)

    left, right = [prepared(side) for side in sides]
    middle = prepared(own)
    target = target_features(own[z.rhs :]).astype(bf16)
    slot = lax.broadcasted_iota(jnp.int32, (z.slots, z.nodes), 0)
    sources = jnp.where(slot < count_ref[...], list_ref[...], -1)
    for level in range(z.levels):
        count, half, first = z.counts[level], halves(z.counts[level]), z.offsets[level]
        at = z.message_c[level] - start
        features, values = [
            jnp.concatenate(
                [
                    left[k][:, at : at + half * rank],
                    middle[k][:, first * rank : (first + count) * rank],
                    right[k][:, at : at + half * rank],
                ],
                axis=1,
            )
            for k in range(2)
        ]
        features = features.T.astype(bf16)
        total = z.ext_counts[level]
        named = jnp.concatenate(
            [
                jnp.broadcast_to(sources[:, first + i : first + i + 1], (z.slots, rank))
                for i in range(count)
            ],
            axis=1,
        )
        here = lax.broadcasted_iota(jnp.int32, (total, count * rank), 0) + device * count - half
        mask = jnp.zeros(here.shape, f32)
        for k in range(z.slots):
            mask = jnp.where(named[k : k + 1] == here, 1.0, mask)
        step = min(4, count)
        for i in range(0, count, step):
            nodes = slice(i, i + step + 2 * half)
            lanes = slice(i * rank, (i + step) * rank)
            rows = slice(i * rank, (i + step + 2 * half) * rank)
            there = slice((first + i) * rank, (first + i + step) * rank)
            matrix = kernel_of(dot(features[rows], target[:, there], 1, 0))
            matrix = matrix.reshape(step + 2 * half, rank, step * rank) * mask[nodes, None, lanes]
            matrix_high, matrix_low = split2(matrix.reshape(-1, step * rank))
            chosen = values[:, rows]
            both = dot(chosen, matrix_high, 1, 0)
            low = dot(chosen[: z.rhs], matrix_low, 1, 0)
            out_ref[:, there] = both[: z.rhs] + both[z.rhs :] + low


def upper_kernels(z, k, level, device, upper_ref, skel_ref):
    anchor = z.anchor(device, level)
    target = target_features(pad8(skel_ref[:, anchor, :])).T.astype(bf16)
    points = []
    for slot in range(z.level_slots(level)):
        source = upper_ref[k * z.slots + slot]
        points.append(pad8(skel_ref[:, jnp.where(source < 0, anchor, source), :]))
    return kernel_of(dot(target, source_features(packed(points)).astype(bf16), 1, 0))


def upper_sources(z, k, level, device, upper_ref, table):
    anchor = z.anchor(device, level)
    coefs = []
    for slot in range(z.level_slots(level)):
        source = upper_ref[k * z.slots + slot]
        coefs.append(table(jnp.where(source < 0, 0, source ^ anchor)) * jnp.where(source < 0, 0.0, GAIN))
    return packed(coefs)


def upper_width(z):
    return sum(z.level_slots(level) for level in z.upper_levels) * z.rank


def top_kernel(z, bounds_ref, upper_ref, skel_ref, matrix_ref, high_ref, low_ref):
    device = bounds_ref[2]
    chain = None
    for k, level in enumerate(z.upper_levels):
        if chain is not None:
            chain = matmul(matrix_ref[z.place(device, level)], chain)
        if z.level_slots(level):
            kernels = upper_kernels(z, k, level, device, upper_ref, skel_ref)
            chain = kernels if chain is None else jnp.concatenate([chain, kernels], axis=1)
    high_ref[...], low_ref[...] = split2(chain)


def mid_kernel(z, fields_ref, basis_ref, transfer_ref, acc_in, acc, weights):
    rank, rhs = z.rank, z.rhs
    row = lax.broadcasted_iota(jnp.int32, (rhs + rank, rank), 0)
    column = lax.broadcasted_iota(jnp.int32, (rhs + rank, rank), 1)
    path = jnp.where(row - rhs == column, 1.0, 0.0)
    none = jnp.zeros((rank, rank), f32)
    path = matmul(path, transfer_ref[z.nodes - 1], 1, 1)
    paths = [path + jnp.concatenate([fields_ref[:, (z.nodes - 1) * rank : z.nodes * rank], none], axis=0)]
    none = jnp.zeros((rank, 2 * rank), f32)
    for level in range(z.levels - 2, -1, -1):
        below = []
        for i, path in enumerate(paths):
            node = z.offsets[level] + 2 * i
            both = matmul(path, transfer_ref[node : node + 2].reshape(2 * rank, rank), 1, 1)
            both += jnp.concatenate([fields_ref[:, node * rank : (node + 2) * rank], none], axis=0)
            below += [both[:, :rank], both[:, rank:]]
        paths = below
    for leaf in range(z.leaves):
        values = matmul(paths[leaf], basis_ref[leaf])
        acc[leaf] += values[:rhs]
        high, low = split2(values[rhs:])
        weights[0, leaf] = high
        weights[1, leaf] = low


def final_kernel(z, bounds_ref, upper_ref, acc, weights, matrix_ref, *rest):
    rest, (out_ref, done_ref, sems) = rest[:-3], rest[-3:]
    tables, (chain_high, chain_low) = rest[:-2], rest[-2:]
    device = bounds_ref[2]
    current = [tables[-1][j] for j in range(z.group)]
    values = {z.top: current}
    for level in range(z.top, 1, -1):
        anchor = z.anchor(device, level)
        moved = [matmul(current[j], matrix_ref[(anchor ^ j) - 4]) for j in range(len(current))]
        current = [moved[2 * j] + moved[2 * j + 1] for j in range(len(current) // 2)]
        values[level - 1] = current
    coefs = []
    for k, level in enumerate(z.upper_levels):
        if z.level_slots(level):

            def table(place, level=level):
                if level >= z.top:
                    return tables[z.depth - 1 - level][place]
                chosen = jnp.zeros((z.rhs, z.rank), f32)
                for j in range(1, len(values[level])):
                    chosen = jnp.where(place == j, values[level][j], chosen)
                return chosen

            coefs.append(upper_sources(z, k, level, device, upper_ref, table))
    downward = couple(chain_high[...], chain_low[...], *split2(packed(coefs)))
    high, low = split2(downward)
    stacked = jnp.concatenate([high, low], axis=0)
    copies = []
    for leaf in range(z.leaves):
        both = dot(stacked, weights[0, leaf], 1, 0)
        value = both[: z.rhs] + both[z.rhs :] + dot(high, weights[1, leaf], 1, 0)
        done_ref[leaf] = acc[leaf] + value
        here = out_ref.at[:, leaf * z.leaf : (leaf + 1) * z.leaf]
        copies.append(pltpu.make_async_copy(done_ref.at[leaf], here, sems.at[leaf]))
        copies[-1].start()
    for copy in copies:
        copy.wait()


SMEM = pl.BlockSpec(memory_space=pltpu.SMEM)
VMEM = pl.BlockSpec(memory_space=pltpu.VMEM)


class Vector:
    def __init__(self, array):
        self.shape, self.dtype = array.shape, array.dtype


def call(body, outs, smem, vmem, scratch=(), aliases=None, cost=1.0, load=False, out_hbm=False):
    many = isinstance(outs, (list, tuple))
    listed = list(outs) if many else [outs]
    places = [
        pltpu.SMEM if o.dtype == jnp.int32 and not isinstance(o, Vector) else pltpu.VMEM for o in listed
    ]
    specs = [pl.BlockSpec(memory_space=pltpu.HBM if out_hbm else place) for place in places]
    shapes = [
        jax.ShapeDtypeStruct(o.shape, o.dtype) if out_hbm else place(o.shape, o.dtype)
        for o, place in zip(listed, places)
    ]
    source = pltpu.HBM if load else pltpu.VMEM
    if not load:
        smem = [pltpu.with_memory_space_constraint(x, pltpu.SMEM) for x in smem]
    vmem = [pltpu.with_memory_space_constraint(x, source) for x in vmem]
    return pl.pallas_call(
        body,
        out_shape=shapes if many else shapes[0],
        in_specs=[SMEM] * len(smem) + [pl.BlockSpec(memory_space=source)] * len(vmem),
        out_specs=specs if many else specs[0],
        scratch_shapes=list(scratch),
        input_output_aliases=aliases or {},
        compiler_params=pltpu.CompilerParams(vmem_limit_bytes=16 << 20),
        cost_estimate=pl.CostEstimate(
            flops=int(cost * 1e8), bytes_accessed=int(cost * 3e6), transcendentals=0
        ),
    )(*smem, *vmem)


def flip(x, axis, bit):
    return lax.ppermute(x, axis, [(i, i ^ bit) for i in range(lax.axis_size(axis))])


def shape(*dims, dtype=f32):
    return jax.ShapeDtypeStruct(dims, dtype)


def on_device(
    right_sides,
    points,
    basis,
    transfer,
    skeleton,
    near_list,
    near_count,
    inter_list,
    inter_count,
    upper_transfer,
    upper_skeleton,
    upper_list,
    upper_count,
):
    z = Sizes(
        lax.axis_size("group"),
        lax.axis_size("bulk"),
        basis.shape[0],
        basis.shape[1],
        basis.shape[2],
        right_sides.shape[0],
        near_list.shape[1],
        inter_list.shape[1],
    )
    part = functools.partial
    integers = part(shape, dtype=jnp.int32)
    halfs = part(shape, dtype=bf16)
    skeleton, upper_skeleton = skeleton.transpose(1, 0, 2), upper_skeleton.transpose(1, 0, 2)
    inter_list, inter_count, upper_list = inter_list.T, inter_count.reshape(1, -1), upper_list.T

    to_partner, to_other, own, term, where, *kept = call(
        part(up_kernel, z),
        [
            shape(z.rhs + 8, z.message_term),
            shape(z.rhs + 8, z.message_term),
            shape(z.rhs + 8, z.packed),
            shape(z.rhs, z.rank),
            integers(1),
            *[integers(*a.shape) for a in (near_list, near_count, upper_list, upper_count)],
            *[shape(*a.shape, dtype=a.dtype) for a in (right_sides, points, basis, transfer)],
            *[Vector(a) for a in (inter_list, inter_count)],
            shape(*upper_skeleton.shape),
            shape(z.shared + z.depth - 1 - z.top, z.rank, z.rank),
        ],
        [],
        [near_list, near_count, upper_list, upper_count, right_sides, points, basis, transfer, skeleton, inter_list, inter_count, upper_skeleton, upper_transfer],
        scratch=[
            pltpu.VMEM(skeleton.shape, f32),
            pltpu.SemaphoreType.DMA((13 + z.depth,)),
        ],
        cost=2.0,
        load=True,
    )
    lists, kept = kept[:4], kept[4:]
    right_sides, points, basis, transfer, inter_list, inter_count, upper_skeleton, matrices = kept
    their_term = flip(term, "bulk", 1)
    from_partner = flip(to_partner, "bulk", 1)
    sources = (2 * z.rhs, z.leaf)
    src, tgt, val, acc = call(
        part(own_kernel, z),
        [
            halfs(z.leaves, z.leaf, FEATURES),
            halfs(z.leaves, FEATURES, z.leaf),
            halfs(z.leaves, *sources),
            shape(z.leaves, z.rhs, z.leaf),
        ],
        [],
        [right_sides, points],
        cost=0.7,
    )
    items, halo_items, bounds, upper = call(
        part(lists_kernel, z),
        [
            integers(z.leaves * (z.near + 1) + 2 * STEP),
            integers(z.leaves * z.near + 2 * STEP),
            integers(3),
            integers(len(z.upper_levels) * z.slots),
        ],
        [where, *lists],
        [],
        cost=0.7,
    )
    terms = call(
        part(pair_kernel, z),
        shape(z.depth - z.top, z.rhs, z.rank),
        [where],
        [term, their_term, matrices],
        cost=0.3,
    )
    pairs = [(i, i + 1) for i in range(1, z.devices - 1, 2)]
    from_other = lax.ppermute(to_other, AXES, pairs + [(b, a) for a, b in pairs])

    whole_levels, partial = [], terms
    for bit in range(1, z.bulk.bit_length() - 1):
        whole_levels.append([partial[:1]])
        partial = partial[1:]
        sizes = [sum(p.shape[0] for p in level) for level in whole_levels]
        sent = jnp.concatenate([p for level in whole_levels for p in level] + [partial], axis=0)
        received = flip(sent, "bulk", 1 << bit)
        at = 0
        for level, size in zip(whole_levels, sizes):
            level.append(received[at : at + size])
            at += size
        partial = partial + received[at:]
    for bit in range(z.top):
        partial = jnp.concatenate([partial, flip(partial, "group", 1 << bit)], axis=0)
    tables = [jnp.concatenate(level, axis=0) for level in whole_levels] + [partial]

    def near(index, acc, more=()):
        arrays = [tgt, src, val, *more, acc]
        return call(
            part(near_kernel, z, index),
            shape(z.leaves, z.rhs, z.leaf),
            [items, halo_items, bounds],
            arrays,
            aliases={2 + len(arrays): 0},
            cost=2.0,
        )

    for index in range(len(NEAR_CUTS)):
        acc = near(index, acc)
    halo_tables = call(
        part(halo_kernel, z),
        [halfs(2 * z.half, z.leaf, FEATURES), halfs(2 * z.half, *sources)],
        [bounds],
        [from_partner, from_other],
        cost=0.5,
    )
    acc = near(len(NEAR_CUTS), acc, halo_tables)
    fields = call(
        part(local_kernel, z),
        shape(z.rhs, z.packed),
        [bounds],
        [inter_list, inter_count, own, from_partner, from_other],
        cost=1.5,
    )
    chain = call(
        part(top_kernel, z),
        [halfs(z.rank, upper_width(z))] * 2,
        [bounds, upper],
        [upper_skeleton, matrices],
        cost=0.6,
    )
    acc, weights = call(
        part(mid_kernel, z),
        [shape(z.leaves, z.rhs, z.leaf), halfs(2, z.leaves, z.rank, z.leaf)],
        [],
        [fields, basis, transfer, acc],
        aliases={3: 0},
        cost=1.0,
    )
    return call(
        part(final_kernel, z),
        shape(*right_sides.shape),
        [bounds, upper],
        [acc, weights, matrices, *tables, *chain],
        scratch=[
            pltpu.VMEM((z.leaves, z.rhs, z.leaf), f32),
            pltpu.SemaphoreType.DMA((z.leaves,)),
        ],
        cost=1.0,
        out_hbm=True,
    )


def solution(mesh):
    in_specs = (
        P(None, AXES),
        P(None, AXES),
        P(AXES, None, None),
        P(AXES, None, None),
        P(AXES, None, None),
        P(AXES, None),
        P(AXES),
        P(AXES, None),
        P(AXES),
        P(),
        P(),
        P(),
        P(),
    )
    return jax.shard_map(
        on_device, mesh=mesh, in_specs=in_specs, out_specs=P(None, AXES), check_vma=False
    )
```

```python
import functools
import math

import jax
import jax.numpy as jnp
from jax import lax
from jax.experimental import pallas as pl
from jax.experimental.pallas import tpu as pltpu
from jax.sharding import PartitionSpec as P


AMPLITUDE = 0.2
KERNEL_RATE = 2.0
SOFTENING = 0.01
NUGGET = 0.5
SCALE = KERNEL_RATE * math.log2(math.e)
FLOOR = SOFTENING * SCALE * SCALE
SHIFT = 1.0 / math.log(2.0)
GAIN = AMPLITUDE * math.log(2.0)
FEATURES = 48
STEP = 8
NEAR_CUTS = (8, 24, 40)
AXES = ("group", "bulk")

f32 = jnp.float32
bf16 = jnp.bfloat16


def dot(a, b, ca, cb):
    return lax.dot_general(a, b, (((ca,), (cb,)), ((), ())), preferred_element_type=f32)


def split2(x):
    high = x.astype(bf16)
    return high, (x - high.astype(f32)).astype(bf16)


def split3(x):
    a = x.astype(bf16).astype(f32)
    b = (x - a).astype(bf16).astype(f32)
    return a, b, x - a - b


def matmul(a, b, ca=1, cb=0):
    ah, al = split2(a)
    bh, bl = split2(b)
    rows = a.shape[1 - ca]
    if ca == 1:
        both = dot(jnp.concatenate([ah, al], axis=0), bh, ca, cb)
        return both[:rows] + both[rows:] + dot(ah, bl, ca, cb)
    return dot(ah, bh, ca, cb) + dot(al, bh, ca, cb) + dot(ah, bl, ca, cb)


def scaled_points(coords):
    u = coords * SCALE
    return u, jnp.broadcast_to(jnp.sum(u * u, axis=0, keepdims=True), u.shape)


def place(row, vector, first, second, third):
    rest = jnp.where(row == 5, third, 0.0)
    rest = jnp.where(row == 4, second, rest)
    rest = jnp.where(row == 3, first, rest)
    return jnp.where(row < 3, vector, rest)


def source_features(coords):
    u, length = scaled_points(coords)
    row = lax.broadcasted_iota(jnp.int32, u.shape, 0)
    a, b, c = split3(u)
    return jnp.concatenate(
        [place(row, a, *split3(length)), place(row, a, 1.0, 1.0, 1.0), b, b, a, c], axis=0
    )


def target_features(coords):
    u, length = scaled_points(coords)
    row = lax.broadcasted_iota(jnp.int32, u.shape, 0)
    a, b, c = split3(-2.0 * u)
    return jnp.concatenate(
        [place(row, a, 1.0, 1.0, 1.0), place(row, b, *split3(length + FLOOR)), a, b, c, a], axis=0
    )


def kernel_of(square):
    t = square * lax.rsqrt(square)
    return (SHIFT + t) * jnp.exp2(-t)


def halves(nodes):
    return max(nodes // 2, 1)


class Sizes:
    def __init__(self, mesh_group, mesh_bulk, leaves, rank, leaf, rhs, near, slots):
        self.group, self.bulk = mesh_group, mesh_bulk
        self.devices = mesh_group * mesh_bulk
        self.leaves, self.rank, self.leaf, self.rhs = leaves, rank, leaf, rhs
        self.near, self.slots = near, slots
        self.levels = leaves.bit_length()
        self.counts = [leaves >> level for level in range(self.levels)]
        self.offsets = [2 * leaves - 2 * count for count in self.counts]
        self.nodes = 2 * leaves - 1
        self.depth = self.devices.bit_length() - 1
        self.top = mesh_group.bit_length() - 1
        self.half = halves(leaves)
        assert 2 * self.half == leaves and leaves & (leaves - 1) == 0
        self.message_c = []
        at = self.half * leaf
        for count in self.counts:
            self.message_c.append(at)
            at += halves(count) * rank
        self.message_term = -(-at // 128) * 128
        self.packed = -(-self.nodes * rank // 128) * 128
        self.upper_levels = list(range(1, self.depth))

    def level_size(self, level):
        return self.bulk >> (self.depth - level) if level > self.top else 1 << level

    def level_slots(self, level):
        return min(self.slots, self.level_size(level) - 1)

    @property
    def shared(self):
        return max(2 * self.group - 4, 0)

    def matrix(self, level):
        return self.shared + level - self.top - 1

    def place(self, device, level):
        return self.matrix(level) if level > self.top else self.anchor(device, level) - 4

    def anchor(self, device, level):
        return (self.devices + device) >> (self.depth - level)


def up_kernel(
    z, near_list_in, near_count_in, upper_list_in, upper_count_in,
    rhs_in, pts_in, basis_in, transfer_in, skel_in, inter_list_in, inter_count_in, upper_skel_in, matrix_in,
    near_msg, far_msg, own_ref, term_ref, where_ref, near_list, near_count, upper_list, upper_count,
    rhs_ref, pts_ref, basis_ref, transfer_ref, inter_list_ref, inter_count_ref, upper_skel_ref, matrix_ref,
    skel_ref, sems,
):
    device = lax.axis_index(AXES[0]) * z.bulk + lax.axis_index(AXES[1])
    moves = [
        (rhs_in, rhs_ref),
        (basis_in, basis_ref),
        (transfer_in, transfer_ref),
        (skel_in, skel_ref),
        (pts_in, pts_ref),
        (near_list_in, near_list),
        (near_count_in, near_count),
        (upper_list_in, upper_list),
        (upper_count_in, upper_count),
        (inter_list_in, inter_list_ref),
        (inter_count_in, inter_count_ref),
        (upper_skel_in, upper_skel_ref),
        (matrix_in.at[4 : 2 * z.group], matrix_ref.at[0 : z.shared]),
    ]
    for level in range(z.top + 1, z.depth):
        moves.append((matrix_in.at[z.anchor(device, level)], matrix_ref.at[z.matrix(level)]))
    copies = [pltpu.make_async_copy(*move, sems.at[i]) for i, move in enumerate(moves)]
    for copy in copies:
        copy.start()
    where_ref[0] = device
    parity = device % 2
    for copy in copies[:2]:
        copy.wait()
    pair = 2 * z.rank
    rows, spare = slice(0, z.rhs), slice(z.rhs, z.rhs + 8)
    coords = slice(z.rhs, z.rhs + 3)
    pieces = []
    for leaf in range(z.leaves):
        at = leaf * z.leaf
        pieces.append(matmul(rhs_ref[:, at : at + z.leaf], basis_ref[leaf], 1, 1))
    for copy in copies[2:]:
        copy.wait()
    own_ref[spare, :] = jnp.zeros((8, z.packed), f32)
    for node in range(z.nodes):
        own_ref[coords, node * z.rank : (node + 1) * z.rank] = skel_ref[:, node, :]
    for level in range(z.levels):
        first = z.offsets[level]
        if len(pieces) == 1:
            own_ref[rows, first * z.rank : (first + 1) * z.rank] = pieces[0]
            break
        raised = []
        for i in range(len(pieces) // 2):
            both = jnp.concatenate([pieces[2 * i], pieces[2 * i + 1]], axis=1)
            node = first + 2 * i
            own_ref[rows, node * z.rank : node * z.rank + pair] = both
            raised.append(matmul(both, transfer_ref[node : node + 2].reshape(pair, z.rank)))
        pieces = raised
    term = matmul(pieces[0], transfer_ref[z.nodes - 1])
    term_ref[...] = term
    width = z.half * z.leaf
    for ref, other in ((near_msg, 0), (far_msg, 1)):
        last = (parity + 1 + other) % 2
        at = pl.multiple_of(last * ((z.leaves - z.half) * z.leaf), 128)
        ref[spare, :] = jnp.zeros((8, ref.shape[1]), f32)
        ref[rows, 0:width] = rhs_ref[:, pl.ds(at, width)]
        ref[coords, 0:width] = pts_ref[:, pl.ds(at, width)]
        for level in range(z.levels):
            size = halves(z.counts[level]) * z.rank
            first = z.offsets[level] * z.rank
            shift = (z.counts[level] - halves(z.counts[level])) * z.rank
            here = slice(z.message_c[level], z.message_c[level] + size)
            low = own_ref[:, first : first + size]
            if shift:
                low = jnp.where(last == 1, own_ref[:, first + shift : first + shift + size], low)
            ref[:, here] = low


def lists_kernel(z, where_ref, near_list, near_count, upper_list, upper_count, items_ref, halo_ref, bounds_ref, upper_ref):
    device = where_ref[0]
    for leaf in range(z.leaves):
        items_ref[leaf] = leaf * (z.leaves + 1)
    here = jnp.int32(z.leaves)
    away = jnp.int32(0)
    base = device * z.leaves
    bits = z.leaves.bit_length() - 1
    for leaf in range(z.leaves):
        count = near_count[leaf]
        for slot in range(z.near):
            source = near_list[leaf, slot] - base
            used = (slot < count).astype(jnp.int32)
            inside = jnp.where(lax.shift_right_arithmetic(source, bits) == 0, used, 0)
            items_ref[here] = source + leaf * z.leaves
            halo_ref[away] = jnp.bitwise_and(source + z.half, 2 * z.half - 1) + leaf * 2 * z.half
            here = here + inside
            away = away + used - inside
    bounds_ref[0] = here
    bounds_ref[1] = away
    bounds_ref[2] = device
    for k, level in enumerate(z.upper_levels):
        anchor = z.anchor(device, level)
        used = upper_count[anchor]
        for slot in range(z.level_slots(level)):
            upper_ref[k * z.slots + slot] = jnp.where(slot < used, upper_list[slot, anchor], -1)


def pair_kernel(z, where_ref, term_ref, a_ref, matrix_ref, out_ref):
    term = term_ref[...] + a_ref[...]
    out_ref[0] = term
    for i, level in enumerate(range(z.depth - 1, z.top, -1)):
        term = matmul(term, matrix_ref[z.matrix(level)])
        out_ref[i + 1] = term


def pad8(block):
    return jnp.concatenate([block, jnp.zeros((8 - block.shape[0], block.shape[1]), f32)], axis=0)


def fill_sources(z, src, val, first, values, coords):
    high, low = split2(values * GAIN)
    features = source_features(coords)
    for i in range(values.shape[1] // z.leaf):
        here = slice(i * z.leaf, (i + 1) * z.leaf)
        val[first + i, 0 : z.rhs] = high[:, here]
        val[first + i, z.rhs : 2 * z.rhs] = low[:, here]
        src[first + i] = features[:, here].T.astype(bf16)


def own_kernel(z, rhs_ref, pts_ref, src, tgt, val, acc):
    coords = pad8(pts_ref[...])
    fill_sources(z, src, val, 0, rhs_ref[...], coords)
    features = target_features(coords).astype(bf16)
    for i in range(z.leaves):
        here = slice(i * z.leaf, (i + 1) * z.leaf)
        tgt[i] = features[:, here]
        acc[i] = NUGGET * rhs_ref[:, here]


def halo_kernel(z, bounds_ref, a_ref, b_ref, src, val):
    width = z.half * z.leaf
    parity = bounds_ref[2] % 2
    left = jnp.where(parity == 0, b_ref[:, 0:width], a_ref[:, 0:width])
    right = jnp.where(parity == 0, a_ref[:, 0:width], b_ref[:, 0:width])
    fill_sources(z, src, val, 0, left[0 : z.rhs], left[z.rhs : z.rhs + 8])
    fill_sources(z, src, val, z.half, right[0 : z.rhs], right[z.rhs : z.rhs + 8])


def run_items(z, list_ref, per_target, first, end, src, tgt, val, acc):
    bits = per_target.bit_length() - 1

    def load(at, size):
        items = [list_ref[at + k] for k in range(size)]
        targets = [lax.shift_right_logical(item, bits) for item in items]
        return targets, [jnp.bitwise_and(item, per_target - 1) for item in items]

    def group(targets, sources):
        for target, source in zip(targets, sources):
            kernel_high, kernel_low = split2(kernel_of(dot(src[source], tgt[target], 1, 0)))
            values = val[source]
            both = dot(values, kernel_high, 1, 0)
            low = dot(values[: z.rhs], kernel_low, 1, 0)
            acc[target] += both[: z.rhs] + both[z.rhs :] + low

    count = end - first
    groups = lax.shift_right_logical(count, STEP.bit_length() - 1)

    def body(i, ready):
        later = load(first + (i + 1) * STEP, STEP)
        group(*ready)
        return later

    lax.fori_loop(0, groups, body, load(first, STEP))
    at = first + groups * STEP
    size = STEP // 2
    while size:
        rest = jnp.bitwise_and(count, size)

        @pl.when(rest != 0)
        def _(at=at, size=size):
            group(*load(at, size))

        at = at + rest
        size //= 2


def near_kernel(z, part, items_ref, halo_ref, bounds_ref, tgt, src, val, *rest):
    here, away = bounds_ref[0], bounds_ref[1]
    cuts = [0] + [jnp.minimum(here, cut) for cut in NEAR_CUTS] + [here]
    begin, end = cuts[part], cuts[part + 1]
    acc = rest[-1]
    run_items(z, items_ref, z.leaves, begin, end, src, tgt, val, acc)
    if part == len(NEAR_CUTS):
        run_items(z, halo_ref, 2 * z.half, 0, away, rest[0], tgt, rest[1], acc)


def packed(blocks):
    return blocks[0] if len(blocks) == 1 else jnp.concatenate(blocks, axis=1)


def couple(kernel_high, kernel_low, high, low):
    rows = high.shape[0]
    both = dot(jnp.concatenate([high, low], axis=0), kernel_high, 1, 1)
    return both[:rows] + both[rows:] + dot(high, kernel_low, 1, 1)


def prepared(z, block):
    high, low = split2(block[: z.rhs] * GAIN)
    features = source_features(block[z.rhs :]).T.astype(bf16)
    return features, jnp.concatenate([high, low], axis=0)


def coupled(z, features, values, target, named, first):
    nodes, lanes = features.shape[0] // z.rank, target.shape[1]
    here = lax.broadcasted_iota(jnp.int32, (nodes, lanes), 0) + first
    mask = jnp.zeros((nodes, lanes), f32)
    for slot in range(z.slots):
        mask = jnp.where(named[slot : slot + 1] == here, 1.0, mask)
    matrix = kernel_of(dot(features, target, 1, 0))
    matrix = matrix.reshape(nodes, z.rank, lanes) * mask[:, None]
    high, low = split2(matrix.reshape(nodes * z.rank, lanes))
    both = dot(values, high, 1, 0)
    return both[: z.rhs] + both[z.rhs :] + dot(values[: z.rhs], low, 1, 0)


def inner_kernel(z, where_ref, list_ref, count_ref, own_ref, out_ref, target_ref, named_ref):
    device = where_ref[0]
    rank = z.rank
    features, values = prepared(z, own_ref[...])
    target_ref[...] = target_features(own_ref[z.rhs :]).astype(bf16)
    slot = lax.broadcasted_iota(jnp.int32, (z.slots, z.nodes), 0)
    sources = jnp.where(slot < count_ref[...], list_ref[...], -1)
    for node in range(z.nodes):
        here = slice(node * rank, (node + 1) * rank)
        named_ref[:, here] = jnp.broadcast_to(sources[:, node : node + 1], (z.slots, rank))
    for level in range(z.levels):
        count, half, first = z.counts[level], halves(z.counts[level]), z.offsets[level]
        step = min(4, count)
        for i in range(0, count, step):
            low, high = max(0, i - half), min(count, i + step + half)
            rows = slice((first + low) * rank, (first + high) * rank)
            there = slice((first + i) * rank, (first + i + step) * rank)
            if count == 1:
                out_ref[:, there] = jnp.zeros((z.rhs, rank), f32)
                continue
            out_ref[:, there] = coupled(
                z, features[rows], values[:, rows], target_ref[:, there], named_ref[:, there], device * count + low
            )


def outer_kernel(z, where_ref, a_ref, b_ref, target_ref, named_ref, fields_in, out_ref):
    device = where_ref[0]
    parity = device % 2
    rank = z.rank
    start, width = z.message_c[0], z.message_term - z.message_c[0]
    a, b = a_ref[:, start : start + width], b_ref[:, start : start + width]
    left = prepared(z, jnp.where(parity == 0, b, a))
    right = prepared(z, jnp.where(parity == 0, a, b))
    for level in range(z.levels):
        count, half, first = z.counts[level], halves(z.counts[level]), z.offsets[level]
        at = z.message_c[level] - start
        rows = slice(at, at + half * rank)
        for (features, values), low, source in (
            (left, 0, device * count - half),
            (right, count - half, (device + 1) * count),
        ):
            there = slice((first + low) * rank, (first + low + half) * rank)
            out_ref[:, there] += coupled(
                z, features[rows], values[:, rows], target_ref[:, there], named_ref[:, there], source
            )


def upper_kernels(z, k, level, device, upper_ref, skel_ref):
    anchor = z.anchor(device, level)
    target = target_features(pad8(skel_ref[:, anchor, :])).T.astype(bf16)
    points = []
    for slot in range(z.level_slots(level)):
        source = upper_ref[k * z.slots + slot]
        points.append(pad8(skel_ref[:, jnp.where(source < 0, anchor, source), :]))
    return kernel_of(dot(target, source_features(packed(points)).astype(bf16), 1, 0))


def upper_sources(z, k, level, device, upper_ref, table):
    anchor = z.anchor(device, level)
    coefs = []
    for slot in range(z.level_slots(level)):
        source = upper_ref[k * z.slots + slot]
        coefs.append(table(jnp.where(source < 0, 0, source ^ anchor)) * jnp.where(source < 0, 0.0, GAIN))
    return packed(coefs)


def upper_width(z):
    return sum(z.level_slots(level) for level in z.upper_levels) * z.rank


def top_kernel(z, bounds_ref, upper_ref, skel_ref, matrix_ref, high_ref, low_ref):
    device = bounds_ref[2]
    chain = None
    for k, level in enumerate(z.upper_levels):
        if chain is not None:
            chain = matmul(matrix_ref[z.place(device, level)], chain)
        if z.level_slots(level):
            kernels = upper_kernels(z, k, level, device, upper_ref, skel_ref)
            chain = kernels if chain is None else jnp.concatenate([chain, kernels], axis=1)
    high_ref[...], low_ref[...] = split2(chain)


def weights_kernel(z, basis_ref, transfer_ref, weights):
    rank = z.rank
    paths = [jnp.transpose(transfer_ref[z.nodes - 1])]
    for level in range(z.levels - 2, -1, -1):
        below = []
        for i, path in enumerate(paths):
            node = z.offsets[level] + 2 * i
            both = matmul(path, transfer_ref[node : node + 2].reshape(2 * rank, rank), 1, 1)
            below += [both[:, :rank], both[:, rank:]]
        paths = below
    for leaf in range(z.leaves):
        weights[0, leaf], weights[1, leaf] = split2(matmul(paths[leaf], basis_ref[leaf]))


def mid_kernel(z, fields_ref, basis_ref, transfer_ref, acc_in, acc):
    rank = z.rank
    paths = [fields_ref[:, (z.nodes - 1) * rank : z.nodes * rank]]
    for level in range(z.levels - 2, -1, -1):
        below = []
        for i, path in enumerate(paths):
            node = z.offsets[level] + 2 * i
            both = matmul(path, transfer_ref[node : node + 2].reshape(2 * rank, rank), 1, 1)
            both += fields_ref[:, node * rank : (node + 2) * rank]
            below += [both[:, :rank], both[:, rank:]]
        paths = below
    for leaf in range(z.leaves):
        acc[leaf] += matmul(paths[leaf], basis_ref[leaf])


def final_kernel(z, bounds_ref, upper_ref, acc, weights, matrix_ref, *rest):
    rest, (out_ref, done_ref, sems) = rest[:-3], rest[-3:]
    tables, (chain_high, chain_low) = rest[:-2], rest[-2:]
    device = bounds_ref[2]
    current = [tables[-1][j] for j in range(z.group)]
    values = {z.top: current}
    for level in range(z.top, 1, -1):
        anchor = z.anchor(device, level)
        moved = [matmul(current[j], matrix_ref[(anchor ^ j) - 4]) for j in range(len(current))]
        current = [moved[2 * j] + moved[2 * j + 1] for j in range(len(current) // 2)]
        values[level - 1] = current
    coefs = []
    for k, level in enumerate(z.upper_levels):
        if z.level_slots(level):

            def table(place, level=level):
                if level >= z.top:
                    return tables[z.depth - 1 - level][place]
                chosen = jnp.zeros((z.rhs, z.rank), f32)
                for j in range(1, len(values[level])):
                    chosen = jnp.where(place == j, values[level][j], chosen)
                return chosen

            coefs.append(upper_sources(z, k, level, device, upper_ref, table))
    downward = couple(chain_high[...], chain_low[...], *split2(packed(coefs)))
    high, low = split2(downward)
    stacked = jnp.concatenate([high, low], axis=0)
    copies = []
    for leaf in range(z.leaves):
        both = dot(stacked, weights[0, leaf], 1, 0)
        value = both[: z.rhs] + both[z.rhs :] + dot(high, weights[1, leaf], 1, 0)
        done_ref[leaf] = acc[leaf] + value
        here = out_ref.at[:, leaf * z.leaf : (leaf + 1) * z.leaf]
        copies.append(pltpu.make_async_copy(done_ref.at[leaf], here, sems.at[leaf]))
        copies[-1].start()
    for copy in copies:
        copy.wait()


SMEM = pl.BlockSpec(memory_space=pltpu.SMEM)
VMEM = pl.BlockSpec(memory_space=pltpu.VMEM)


class Vector:
    def __init__(self, array):
        self.shape, self.dtype = array.shape, array.dtype


def call(body, outs, smem, vmem, scratch=(), aliases=None, cost=1.0, load=False, out_hbm=False):
    many = isinstance(outs, (list, tuple))
    listed = list(outs) if many else [outs]
    places = [
        pltpu.SMEM if o.dtype == jnp.int32 and not isinstance(o, Vector) else pltpu.VMEM for o in listed
    ]
    specs = [pl.BlockSpec(memory_space=pltpu.HBM if out_hbm else place) for place in places]
    shapes = [
        jax.ShapeDtypeStruct(o.shape, o.dtype) if out_hbm else place(o.shape, o.dtype)
        for o, place in zip(listed, places)
    ]
    source = pltpu.HBM if load else pltpu.VMEM
    if not load:
        smem = [pltpu.with_memory_space_constraint(x, pltpu.SMEM) for x in smem]
    vmem = [pltpu.with_memory_space_constraint(x, source) for x in vmem]
    return pl.pallas_call(
        body,
        out_shape=shapes if many else shapes[0],
        in_specs=[SMEM] * len(smem) + [pl.BlockSpec(memory_space=source)] * len(vmem),
        out_specs=specs if many else specs[0],
        scratch_shapes=list(scratch),
        input_output_aliases=aliases or {},
        compiler_params=pltpu.CompilerParams(vmem_limit_bytes=16 << 20),
        cost_estimate=pl.CostEstimate(
            flops=int(cost * 1e8), bytes_accessed=int(cost * 3e6), transcendentals=0
        ),
    )(*smem, *vmem)


def flip(x, axis, bit):
    return lax.ppermute(x, axis, [(i, i ^ bit) for i in range(lax.axis_size(axis))])


def shape(*dims, dtype=f32):
    return jax.ShapeDtypeStruct(dims, dtype)


def on_device(
    right_sides,
    points,
    basis,
    transfer,
    skeleton,
    near_list,
    near_count,
    inter_list,
    inter_count,
    upper_transfer,
    upper_skeleton,
    upper_list,
    upper_count,
):
    z = Sizes(
        lax.axis_size("group"),
        lax.axis_size("bulk"),
        basis.shape[0],
        basis.shape[1],
        basis.shape[2],
        right_sides.shape[0],
        near_list.shape[1],
        inter_list.shape[1],
    )
    part = functools.partial
    integers = part(shape, dtype=jnp.int32)
    halfs = part(shape, dtype=bf16)
    skeleton, upper_skeleton = skeleton.transpose(1, 0, 2), upper_skeleton.transpose(1, 0, 2)
    inter_list, inter_count, upper_list = inter_list.T, inter_count.reshape(1, -1), upper_list.T

    to_partner, to_other, own, term, where, *kept = call(
        part(up_kernel, z),
        [
            shape(z.rhs + 8, z.message_term),
            shape(z.rhs + 8, z.message_term),
            shape(z.rhs + 8, z.packed),
            shape(z.rhs, z.rank),
            integers(1),
            *[integers(*a.shape) for a in (near_list, near_count, upper_list, upper_count)],
            *[shape(*a.shape, dtype=a.dtype) for a in (right_sides, points, basis, transfer)],
            *[Vector(a) for a in (inter_list, inter_count)],
            shape(*upper_skeleton.shape),
            shape(z.shared + z.depth - 1 - z.top, z.rank, z.rank),
        ],
        [],
        [near_list, near_count, upper_list, upper_count, right_sides, points, basis, transfer, skeleton, inter_list, inter_count, upper_skeleton, upper_transfer],
        scratch=[
            pltpu.VMEM(skeleton.shape, f32),
            pltpu.SemaphoreType.DMA((13 + z.depth,)),
        ],
        cost=2.0,
        load=True,
    )
    lists, kept = kept[:4], kept[4:]
    right_sides, points, basis, transfer, inter_list, inter_count, upper_skeleton, matrices = kept
    their_term = flip(term, "bulk", 1)
    from_partner = flip(to_partner, "bulk", 1)
    sources = (2 * z.rhs, z.leaf)
    src, tgt, val, acc = call(
        part(own_kernel, z),
        [
            halfs(z.leaves, z.leaf, FEATURES),
            halfs(z.leaves, FEATURES, z.leaf),
            halfs(z.leaves, *sources),
            shape(z.leaves, z.rhs, z.leaf),
        ],
        [],
        [right_sides, points],
        cost=0.7,
    )
    items, halo_items, bounds, upper = call(
        part(lists_kernel, z),
        [
            integers(z.leaves * (z.near + 1) + 2 * STEP),
            integers(z.leaves * z.near + 2 * STEP),
            integers(3),
            integers(len(z.upper_levels) * z.slots),
        ],
        [where, *lists],
        [],
        cost=0.7,
    )
    terms = call(
        part(pair_kernel, z),
        shape(z.depth - z.top, z.rhs, z.rank),
        [where],
        [term, their_term, matrices],
        cost=0.3,
    )
    pairs = [(i, i + 1) for i in range(1, z.devices - 1, 2)]
    from_other = lax.ppermute(to_other, AXES, pairs + [(b, a) for a, b in pairs])

    whole_levels, partial = [], terms
    for bit in range(1, z.bulk.bit_length() - 1):
        whole_levels.append([partial[:1]])
        partial = partial[1:]
        sizes = [sum(p.shape[0] for p in level) for level in whole_levels]
        sent = jnp.concatenate([p for level in whole_levels for p in level] + [partial], axis=0)
        received = flip(sent, "bulk", 1 << bit)
        at = 0
        for level, size in zip(whole_levels, sizes):
            level.append(received[at : at + size])
            at += size
        partial = partial + received[at:]
    order = [0]
    for bit in reversed(range(z.top)):
        partial = jnp.concatenate([partial, flip(partial, "group", 1 << bit)], axis=0)
        order += [place ^ 1 << bit for place in order]
    places = [order.index(place) for place in range(z.group)]
    partial = jnp.concatenate([partial[i : i + 1] for i in places], axis=0)
    tables = [jnp.concatenate(level, axis=0) for level in whole_levels] + [partial]

    def near(index, acc, more=()):
        arrays = [tgt, src, val, *more, acc]
        return call(
            part(near_kernel, z, index),
            shape(z.leaves, z.rhs, z.leaf),
            [items, halo_items, bounds],
            arrays,
            aliases={2 + len(arrays): 0},
            cost=2.0,
        )

    for index in range(len(NEAR_CUTS)):
        acc = near(index, acc)
    halo_tables = call(
        part(halo_kernel, z),
        [halfs(2 * z.half, z.leaf, FEATURES), halfs(2 * z.half, *sources)],
        [bounds],
        [from_partner, from_other],
        cost=0.5,
    )
    acc = near(len(NEAR_CUTS), acc, halo_tables)
    fields, target_rows, named = call(
        part(inner_kernel, z),
        [shape(z.rhs, z.packed), halfs(FEATURES, z.packed), Vector(integers(z.slots, z.packed))],
        [where],
        [inter_list, inter_count, own],
        cost=1.0,
    )
    fields = call(
        part(outer_kernel, z),
        shape(z.rhs, z.packed),
        [where],
        [from_partner, from_other, target_rows, named, fields],
        aliases={5: 0},
        cost=0.8,
    )
    chain = call(
        part(top_kernel, z),
        [halfs(z.rank, upper_width(z))] * 2,
        [bounds, upper],
        [upper_skeleton, matrices],
        cost=0.6,
    )
    weights = call(
        part(weights_kernel, z), halfs(2, z.leaves, z.rank, z.leaf), [], [basis, transfer], cost=0.8
    )
    acc = call(
        part(mid_kernel, z),
        shape(z.leaves, z.rhs, z.leaf),
        [],
        [fields, basis, transfer, acc],
        aliases={3: 0},
        cost=0.6,
    )
    return call(
        part(final_kernel, z),
        shape(*right_sides.shape),
        [bounds, upper],
        [acc, weights, matrices, *tables, *chain],
        scratch=[
            pltpu.VMEM((z.leaves, z.rhs, z.leaf), f32),
            pltpu.SemaphoreType.DMA((z.leaves,)),
        ],
        cost=1.0,
        out_hbm=True,
    )


def solution(mesh):
    in_specs = (
        P(None, AXES),
        P(None, AXES),
        P(AXES, None, None),
        P(AXES, None, None),
        P(AXES, None, None),
        P(AXES, None),
        P(AXES),
        P(AXES, None),
        P(AXES),
        P(),
        P(),
        P(),
        P(),
    )
    return jax.shard_map(
        on_device, mesh=mesh, in_specs=in_specs, out_specs=P(None, AXES), check_vma=False
    )
```
